128 devices in a mesh: node: 32 (over x, y, core), local: 4 (over z).
Axes of the slice: x: 4, y: 4, z: 4, core: 2. Of those that a mesh axis runs over, the one named last changes fastest.
Arguments:
- tokens: bfloat16 [16384, 2048], P(('node', 'local')), may hold values from -6 to 6
- route: int32 [16384, 4], P(('node', 'local')), may hold values from 0 to 63, all different within a row; in each aligned block of 128 rows (0 to 127, 128 to 255, ...) at most 9 rows name the same one
- combine_weights: float32 [16384, 4], P(('node', 'local')), may hold values from 0.05 to 1
- w_gate: bfloat16 [64, 2048, 1408], P('node', None, 'local'), may hold values from -0.125 to 0.125
- w_up: bfloat16 [64, 2048, 1408], P('node', None, 'local'), may hold values from -0.125 to 0.125
- w_down: bfloat16 [64, 1408, 2048], P('node', 'local'), may hold values from -0.15625 to 0.15625
- grad_out: bfloat16 [16384, 2048], P(('node', 'local')), may hold values from -6 to 6
Outputs:
- combined: bfloat16 [16384, 2048], P(('node', 'local'))
- d_tokens: bfloat16 [16384, 2048], P(('node', 'local'))
- d_weights: float32 [16384, 4], P(('node', 'local'))
The draws below stay inside these ranges and needn't reach their ends.
Inputs may be any that keep to these rules, and one draw needn't show every extreme that they name: `route`: the 4 experts of one token differ; within the 128 tokens of one device no expert is named more than 9 times, and some device names some expert exactly 9 times.
All inputs are finite; a program needn't handle non-finite values.
Results may differ from the reference program's by a relative error of at most 0.012.
Values may be sent and summed in bfloat16 or wider, within the bound.
No kernel may reach another device: no remote copies, remote signals or barrier semaphores. Data moves between devices by JAX's collectives and lax.ppermute only.
A program may use at most 192 MiB of HBM per device.

```python
import math
import jax
import jax.numpy as jnp
import numpy as np
from jax import lax

D = 2048
FF = 1408
EXPERTS = 64
TOP = 4
TOK_DEV = 128
CAP = 9
TOKENS = 16384
HID = 352


def levels(stream_key, extent, shards, least, high):
    level, own = 1.0, jax.random.fold_in(stream_key, 6)
    for axis_at, blocks in shards:
        draws = jnp.exp(jax.random.uniform(jax.random.fold_in(own, axis_at), (blocks,), jnp.float32, least / len(shards), high / len(shards)))
        level = level * jnp.repeat(draws, extent[axis_at] // blocks).reshape([-1 if axis == axis_at else 1 for axis in range(len(extent))])
    return level


def shared_out(key, own, number, rows, count, top, most, lean):
    sequence = jax.random.permutation(key, count)
    packed, usual = shares(count, rows * top, most, lean, True), shares(count, rows * top, most, lean, False)
    places = jnp.arange(count)

    def named(lengths, rotation):
        used = int((lengths > 0).sum())
        fixed = max(1, used // 4)
        shifted = fixed + (places - fixed + rotation * (used - fixed)) % max(1, count - fixed)
        return jnp.zeros((count,), jnp.int32).at[sequence[jnp.where(places < fixed, places, shifted)]].set(jnp.asarray(lengths, jnp.int32))

    lengths = jnp.where(number % 4 == 0, named(packed, number // 4), named(usual, number - number // 4 - 1))
    mixed = jax.random.permutation(jax.random.fold_in(own, 3), count)
    source_of, taker = mixed[0:count // 2 * 2:2], mixed[1:count // 2 * 2:2]
    room = jnp.minimum(lengths[source_of] - 1, most - lengths[taker]) // 2
    room = jnp.where((source_of == sequence[0]) | (taker == sequence[0]) | (lengths[taker] == 0), 0, jnp.maximum(room, 0))
    shifted = jax.random.randint(jax.random.fold_in(own, 4), (count // 2,), 0, 1 << 20) % (room + 1)
    lengths = lengths.at[source_of].add(-shifted).at[taker].add(shifted)
    members = jnp.searchsorted(jnp.cumsum(lengths), jnp.arange(rows * top), side="right").astype(jnp.int32)
    table = members.reshape(top, rows).T
    table = table[jax.random.permutation(jax.random.fold_in(own, 1), rows)]
    rotation = jax.random.randint(jax.random.fold_in(own, 2), (rows, 1), 0, top)
    return jnp.take_along_axis(table, (jnp.arange(top)[None, :] + rotation) % top, axis=1)


def shares(count, total, most, lean, full):
    weights = [(1 << 20) // math.isqrt(rank ** lean) + 1 for rank in range(1, count + 1)]
    largest = most if full else min(most, max(-(-total // count), total * weights[0] // sum(weights)))
    least = 1 if total - largest >= count - 1 else 0
    holding, spare = [largest] + [least] * (count - 1), total - largest - least * (count - 1)
    while spare > 0:
        candidates = [i for i in range(1, count) if holding[i] < largest] or [i for i in range(1, count) if holding[i] < most]
        pool, budget = sum([weights[i] for i in candidates]), spare
        for i in candidates:
            extra = min(most - holding[i], max(1, budget * weights[i] // pool), spare)
            holding[i] = holding[i] + extra
            spare = spare - extra
    return np.array(holding)


def scatter_about(rng, shape, scale, limit, split=(), kind=jnp.bfloat16):
    loudness = levels(rng, shape, split, -0.22, 0.18) if split else 1.0
    array = jax.random.normal(rng, shape, jnp.float32) * scale * loudness
    return jnp.minimum(jnp.maximum(array, -limit), limit).astype(kind)


def setup_inputs(seed: int = 0) -> dict:
    keys = jax.random.split(jax.random.key(seed), 8)
    tokens = scatter_about(keys[0], (TOKENS, D), 1.0, 6.0, ((0, 128),))
    route_keys = jax.random.split(jax.random.fold_in(keys[1], 1), TOKENS // TOK_DEV)
    route_turns = jax.random.permutation(jax.random.fold_in(keys[1], 3), TOKENS // TOK_DEV)
    route = jax.vmap(lambda own, number: shared_out(jax.random.fold_in(keys[1], 2), own, number, TOK_DEV, EXPERTS, TOP, CAP, 2))(route_keys, route_turns).reshape((TOKENS, TOP))
    combine_weights = jnp.clip(0.05 + 0.95 * jax.random.uniform(keys[2], (TOKENS, TOP), jnp.float32) ** levels(keys[2], (TOKENS, TOP), ((0, 128),), -0.2, 0.2), 0.05, 1.0)
    w_gate = scatter_about(keys[3], (EXPERTS, D, FF), D ** -0.5, 0.125, ((0, 32), (2, 4)))
    w_up = scatter_about(keys[4], (EXPERTS, D, FF), D ** -0.5, 0.125, ((0, 32), (2, 4)))
    w_down = scatter_about(keys[5], (EXPERTS, FF, D), FF ** -0.5, 0.15625, ((0, 32), (1, 4)))
    grad_out = scatter_about(keys[6], (TOKENS, D), 1.0, 6.0, ((0, 128),))
    return dict(tokens=tokens, route=route, combine_weights=combine_weights, w_gate=w_gate, w_up=w_up, w_down=w_down, grad_out=grad_out)


def place_pairs(route_block):
    flat_routes = route_block.reshape(-1)
    one_hot = (flat_routes[:, None] == jnp.arange(EXPERTS, dtype=jnp.int32)[None, :]).astype(jnp.int32)
    earlier = jnp.cumsum(one_hot, axis=0) - one_hot
    slot_rank = jnp.sum(earlier * one_hot, axis=1)
    return (flat_routes * CAP + slot_rank).astype(jnp.int32)


def round_trip(value):
    return lax.optimization_barrier(value.astype(jnp.bfloat16)).astype(jnp.float32)


def one_expert(expert_args):
    token_rows, grad_rows, gate_weight, up_weight, down_weight = expert_args
    gate_val = jnp.dot(token_rows, gate_weight, preferred_element_type=jnp.float32)
    up_val = jnp.dot(token_rows, up_weight, preferred_element_type=jnp.float32)
    hidden = (jax.nn.silu(gate_val) * up_val).astype(jnp.bfloat16)
    d_hidden = jnp.dot(grad_rows, down_weight.T, preferred_element_type=jnp.float32)
    sigmoid_gate = jax.nn.sigmoid(gate_val)
    d_gate = (d_hidden * up_val * sigmoid_gate * (1.0 + gate_val * (1.0 - sigmoid_gate))).astype(jnp.bfloat16)
    d_up = (d_hidden * gate_val * sigmoid_gate).astype(jnp.bfloat16)
    out_total = jnp.zeros((token_rows.shape[0], D), jnp.float32)
    back_total = jnp.zeros((token_rows.shape[0], D), jnp.float32)
    for block_index in range(FF // HID):
        lower_edge = block_index * HID
        upper_edge = lower_edge + HID
        out_total = out_total + round_trip(jnp.dot(hidden[:, lower_edge:upper_edge], down_weight[lower_edge:upper_edge], preferred_element_type=jnp.float32))
        back_term = jnp.dot(d_gate[:, lower_edge:upper_edge], gate_weight[:, lower_edge:upper_edge].T, preferred_element_type=jnp.float32) + jnp.dot(d_up[:, lower_edge:upper_edge], up_weight[:, lower_edge:upper_edge].T, preferred_element_type=jnp.float32)
        back_total = back_total + round_trip(back_term)
    return out_total.astype(jnp.bfloat16), back_total.astype(jnp.bfloat16)


def reference(tokens, route, combine_weights, w_gate, w_up, w_down, grad_out):
    devices = TOKENS // TOK_DEV
    pair_count = TOK_DEV * TOP
    tok_blocks = tokens.reshape(devices, TOK_DEV, D)
    position = jax.vmap(place_pairs)(route.reshape(devices, pair_count))
    dev_index = jnp.arange(devices, dtype=jnp.int32)[:, None]
    pair_tokens = jnp.repeat(tok_blocks, TOP, axis=1)
    buffer_x = jnp.zeros((devices, EXPERTS * CAP, D), jnp.bfloat16).at[dev_index, position].set(pair_tokens)
    weight_blocks = combine_weights.reshape(devices, TOK_DEV, TOP)
    grad_blocks = grad_out.reshape(devices, TOK_DEV, D)
    grad_pairs = (weight_blocks[:, :, :, None] * grad_blocks[:, :, None, :].astype(jnp.float32)).astype(jnp.bfloat16).reshape(devices, pair_count, D)
    buffer_g = jnp.zeros((devices, EXPERTS * CAP, D), jnp.bfloat16).at[dev_index, position].set(grad_pairs)
    by_expert_x = buffer_x.reshape(devices, EXPERTS, CAP, D).transpose(1, 0, 2, 3).reshape(EXPERTS, devices * CAP, D)
    by_expert_g = buffer_g.reshape(devices, EXPERTS, CAP, D).transpose(1, 0, 2, 3).reshape(EXPERTS, devices * CAP, D)
    expert_out, expert_back = lax.map(one_expert, (by_expert_x, by_expert_g, w_gate, w_up, w_down))
    out_rows = expert_out.reshape(EXPERTS, devices, CAP, D).transpose(1, 0, 2, 3).reshape(devices, EXPERTS * CAP, D)
    back_rows = expert_back.reshape(EXPERTS, devices, CAP, D).transpose(1, 0, 2, 3).reshape(devices, EXPERTS * CAP, D)
    pair_out = jnp.take_along_axis(out_rows, position[:, :, None], axis=1).reshape(devices, TOK_DEV, TOP, D).astype(jnp.float32)
    pair_back = jnp.take_along_axis(back_rows, position[:, :, None], axis=1).reshape(devices, TOK_DEV, TOP, D).astype(jnp.float32)
    combined = jnp.sum(weight_blocks[:, :, :, None] * pair_out, axis=2).astype(jnp.bfloat16).reshape(TOKENS, D)
    d_weights = jnp.einsum("ntkd,ntd->ntk", pair_out, grad_blocks.astype(jnp.float32), precision=lax.Precision.HIGHEST).reshape(TOKENS, TOP)
    d_tokens = jnp.sum(pair_back, axis=2).astype(jnp.bfloat16).reshape(TOKENS, D)
    return combined, d_tokens, d_weights
```

```python
import jax
import jax.numpy as jnp
from jax import lax
from jax.sharding import PartitionSpec as P

EXPERTS = 64
TOP = 4
CAP = 9
BF = jnp.bfloat16
F32 = jnp.float32

IN_ROWS = 56
OUT0_ROWS = 40
OUT1_ROWS = 24


def slots_of(route_t):
    toks = route_t.shape[1]
    expert_ids = jnp.arange(EXPERTS, dtype=jnp.int32)[:, None]
    hits = [(route_t[k][None, :] == expert_ids) for k in range(TOP)]
    named = sum(h.astype(BF) for h in hits)
    before = (
        jnp.arange(toks, dtype=jnp.int32)[:, None] < jnp.arange(toks, dtype=jnp.int32)[None, :]
    ).astype(BF)
    earlier = jnp.dot(named, before, preferred_element_type=F32)
    slots = [jnp.sum(jnp.where(h, earlier, 0.0), axis=0) for h in hits]
    return jnp.stack(slots).astype(jnp.int32)


def one_hot_rows(row_t, rows, values=None):
    ids = jnp.arange(rows, dtype=jnp.int32)[:, None]
    total = 0
    for k in range(TOP):
        hit = row_t[k][None, :] == ids
        value = jnp.ones((), F32) if values is None else values[k][None, :]
        total = total + jnp.where(hit, value, 0.0)
    return total.astype(BF)


def shards(tokens, route, combine_weights, w_gate, w_up, w_down, grad_out):
    nodes = lax.axis_size("node")
    planes = lax.axis_size("local")
    toks, width = tokens.shape
    up = [(i, (i + 1) % planes) for i in range(planes)]
    down = [(i, (i - 1) % planes) for i in range(planes)]
    across = [(i, (i + 2) % planes) for i in range(planes)]

    def send(value, pairs):
        return lax.ppermute(value, "local", pairs)

    own = jnp.concatenate([tokens, grad_out], axis=0)
    other = send(own, across)
    route_t = route.T
    weight_t = combine_weights.T
    small = send(jnp.concatenate([weight_t, route_t.astype(F32)], axis=0), across)
    weight_other = small[:TOP]
    route_other = small[TOP:].astype(jnp.int32)

    gate_t = jnp.swapaxes(w_gate, 1, 2)
    up_t = jnp.swapaxes(w_up, 1, 2)
    half = gate_t.shape[1] // 2

    def piece(expert, part):
        cut = slice(part * half, (part + 1) * half)
        return jnp.stack([gate_t[expert, cut], up_t[expert, cut], w_down[expert, cut]])

    p0a, p0b, p1a, p1b = piece(0, 0), piece(0, 1), piece(1, 0), piece(1, 1)
    w0 = jnp.concatenate([p0a, p0b, send(p0a, down), send(p0b, up)], axis=1)
    below_a, below_b = send(p1a, up), send(p1b, up)
    above_a, above_b = send(p1a, down), send(p1b, down)
    far_a, far_b = send(below_a, up), send(above_b, down)
    w1 = jnp.concatenate([p1a, p1b, below_a, below_b, above_a, above_b, far_a, far_b], axis=1)

    def rows_of(route_rows, chunk, base0, base1):
        slot = slots_of(route_rows)
        node = route_rows // 2
        odd = route_rows % 2
        base = jnp.where(odd == 0, base0, base1)
        return jnp.where(base < 0, -1, node * chunk + base + slot)

    send_rows = jnp.dot(
        jnp.concatenate(
            [
                one_hot_rows(rows_of(route_t, IN_ROWS, 0, 36), nodes * IN_ROWS),
                one_hot_rows(rows_of(route_t, IN_ROWS, 18, 45), nodes * IN_ROWS),
                one_hot_rows(rows_of(route_other, IN_ROWS, 9, -1), nodes * IN_ROWS),
                one_hot_rows(rows_of(route_other, IN_ROWS, 27, -1), nodes * IN_ROWS),
            ],
            axis=1,
        ),
        jnp.concatenate([own, other], axis=0),
        preferred_element_type=F32,
    ).astype(BF)

    def exchange(rows):
        return lax.all_to_all(rows, "node", split_axis=0, concat_axis=0, tiled=True)

    arrived = exchange(send_rows).reshape(nodes, IN_ROWS, width)

    def expert(x_rows, g_rows, weights):
        w_g, w_u, w_d = weights[0], weights[1], weights[2]

        def by_hidden(rows, w):
            return lax.dot_general(rows, w, (((1,), (1,)), ((), ())), preferred_element_type=F32)

        gate, upper = by_hidden(x_rows, w_g), by_hidden(x_rows, w_u)
        d_hidden = by_hidden(g_rows, w_d)
        s = jax.nn.sigmoid(gate)
        hidden = (gate * s * upper).astype(BF)
        d_gate = (d_hidden * upper * s * (1.0 + gate * (1.0 - s))).astype(BF)
        d_up = (d_hidden * gate * s).astype(BF)
        out = jnp.dot(hidden, w_d, preferred_element_type=F32)
        back = jnp.dot(d_gate, w_g, preferred_element_type=F32) + jnp.dot(
            d_up, w_u, preferred_element_type=F32
        )
        return out.astype(BF), back.astype(BF)

    def cut(first, count):
        return arrived[:, first : first + count].reshape(nodes * count, width)

    def returned(out, back, count, chunk):
        parts = [out.reshape(nodes, count, width), back.reshape(nodes, count, width)]
        fill = jnp.zeros((nodes, chunk - 2 * count, width), BF)
        return exchange(jnp.concatenate(parts + [fill], axis=1).reshape(nodes * chunk, width))

    out0, back0 = expert(cut(0, 18), cut(18, 18), w0)
    home0 = returned(out0, back0, 18, OUT0_ROWS)
    out1, back1 = expert(cut(36, 9), cut(45, 9), w1)
    home1 = returned(out1, back1, 9, OUT1_ROWS)

    def mix(rows, route_rows, values, chunk, base0, base1):
        matrix = one_hot_rows(
            rows_of(route_rows, chunk, base0, base1), nodes * chunk, values
        )
        return lax.dot_general(matrix, rows, (((0,), (0,)), ((), ())), preferred_element_type=F32)

    def weight_grads(rows, grads, route_rows, chunk, base0, base1):
        row_t = rows_of(route_rows, chunk, base0, base1)
        table = lax.dot_general(
            rows, grads, (((1,), (1,)), ((), ())), preferred_element_type=F32
        )
        ids = jnp.arange(nodes * chunk, dtype=jnp.int32)[:, None]
        return jnp.stack(
            [
                jnp.sum(jnp.where(row_t[k][None, :] == ids, table, 0.0), axis=0)
                for k in range(TOP)
            ]
        )

    back_block = jnp.concatenate(
        [
            mix(home0, route_other, weight_other, OUT0_ROWS, 9, -1),
            mix(home0, route_other, weight_other, OUT0_ROWS, 27, -1),
        ],
        axis=0,
    ).astype(BF)
    returned_block = send(back_block, across).astype(F32)
    returned_dw = send(
        weight_grads(home0, other[toks:], route_other, OUT0_ROWS, 9, -1), across
    )
    combined = (
        mix(home0, route_t, weight_t, OUT0_ROWS, 0, -1)
        + mix(home1, route_t, weight_t, OUT1_ROWS, -1, 0)
        + returned_block[:toks]
    ).astype(BF)
    d_tokens = (
        mix(home0, route_t, weight_t, OUT0_ROWS, 18, -1)
        + mix(home1, route_t, weight_t, OUT1_ROWS, -1, 9)
        + returned_block[toks:]
    ).astype(BF)
    d_weights = (
        weight_grads(home0, grad_out, route_t, OUT0_ROWS, 0, -1)
        + weight_grads(home1, grad_out, route_t, OUT1_ROWS, -1, 0)
        + returned_dw
    ).T
    return combined, d_tokens, d_weights


def solution(mesh):
    tokens_spec = P(("node", "local"), None)
    return jax.shard_map(
        shards,
        mesh=mesh,
        in_specs=(
            tokens_spec,
            tokens_spec,
            tokens_spec,
            P("node", None, "local"),
            P("node", None, "local"),
            P("node", "local", None),
            tokens_spec,
        ),
        out_specs=(tokens_spec, tokens_spec, tokens_spec),
        check_vma=False,
    )
```

```python
import functools

import jax
import jax.numpy as jnp
from jax import lax
from jax.experimental import pallas as pl
from jax.experimental.pallas import tpu as pltpu
from jax.sharding import PartitionSpec as P

EXPERTS = 64
TOP = 4
CAP = 9
BF = jnp.bfloat16
F32 = jnp.float32

IN_ROWS = 56
OUT0_ROWS = 40
OUT1_ROWS = 24


def slots_of(route_t):
    toks = route_t.shape[1]
    expert_ids = jnp.arange(EXPERTS, dtype=jnp.int32)[:, None]
    hits = [(route_t[k][None, :] == expert_ids) for k in range(TOP)]
    named = sum(h.astype(BF) for h in hits)
    before = (
        jnp.arange(toks, dtype=jnp.int32)[:, None] < jnp.arange(toks, dtype=jnp.int32)[None, :]
    ).astype(BF)
    earlier = jnp.dot(named, before, preferred_element_type=F32)
    slots = [jnp.sum(jnp.where(h, earlier, 0.0), axis=0) for h in hits]
    return jnp.stack(slots).astype(jnp.int32)


def one_hot_rows(row_t, rows):
    ids = jnp.arange(rows, dtype=jnp.int32)[:, None]
    total = 0
    for k in range(TOP):
        total = total + jnp.where(row_t[k][None, :] == ids, 1.0, 0.0)
    return total.astype(BF)


def expert_kernel(
    nodes, main, extra, in_rows, out_rows, x_at, g_at, rest_at, x_rest, g_rest, blocks, n_pieces, *refs
):
    arrived, pieces, home = refs[0], refs[1 : 1 + n_pieces], refs[1 + n_pieces]
    xs, gs, rest, wg, wu, wd, outs, backs, out_rest, sems = refs[2 + n_pieces :]
    spread = nodes * 8
    count = nodes * main
    part = pieces[0].shape[1]

    def fetch(first, size, dst, sem):
        def step(n, carry):
            src = arrived.at[pl.ds(pl.multiple_of(n * in_rows + first, 8), size)]
            to = dst.at[pl.ds(pl.multiple_of(n * size, 8), size)]
            pltpu.make_async_copy(src, to, sem).start()
            return carry

        lax.fori_loop(0, nodes, step, 0)

    def landed(dst, sem):
        pltpu.make_async_copy(dst, dst, sem).wait()

    fetch(x_at, main, xs, sems.at[0])
    fetch(rest_at, 8, rest, sems.at[1])
    for j, w in enumerate((wg, wu, wd)):
        for i, p in enumerate(pieces):
            pltpu.make_async_copy(p.at[j], w.at[pl.ds(i * part, part)], sems.at[3 + j]).start()
        if j == 1:
            fetch(g_at, main, gs, sems.at[2])

    small = nodes * extra

    def picked(offset, out_major):
        shape = (small, spread) if not out_major else (spread, small)
        compact = lax.broadcasted_iota(jnp.int32, shape, 1 if out_major else 0)
        wide = lax.broadcasted_iota(jnp.int32, shape, 0 if out_major else 1)
        want = (compact // extra) * 8 + offset + compact % extra
        return (want == wide).astype(F32).astype(BF)

    landed(rest, sems.at[1])
    landed(xs.at[pl.ds(0, count)], sems.at[0])
    xs[pl.ds(count, small)] = jnp.dot(picked(x_rest, False), rest[...], preferred_element_type=F32).astype(BF)
    gs[pl.ds(count, small)] = jnp.dot(picked(g_rest, False), rest[...], preferred_element_type=F32).astype(BF)
    landed(wg, sems.at[3])
    landed(wu, sems.at[4])
    landed(gs.at[pl.ds(0, count)], sems.at[2])
    landed(wd, sems.at[5])

    size = (count + small) // blocks

    def by_hidden(rows, w):
        return lax.dot_general(rows, w, (((1,), (1,)), ((), ())), preferred_element_type=F32)

    def block(b, carry):
        at = pl.ds(pl.multiple_of(b * size, 16), size)
        x = xs[at]
        gate = by_hidden(x, wg[...])
        upper = by_hidden(x, wu[...])
        d_hidden = by_hidden(gs[at], wd[...])
        s = jax.nn.sigmoid(gate)
        act = gate * s
        hidden = (act * upper).astype(BF)
        d_gate = (d_hidden * upper * s * (1.0 + gate * (1.0 - s))).astype(BF)
        d_up = (d_hidden * act).astype(BF)
        outs[at] = jnp.dot(hidden, wd[...], preferred_element_type=F32).astype(BF)
        backs[at] = (
            jnp.dot(d_gate, wg[...], preferred_element_type=F32)
            + jnp.dot(d_up, wu[...], preferred_element_type=F32)
        ).astype(BF)
        return carry

    lax.fori_loop(0, blocks, block, 0)
    out_rest[...] = (
        jnp.dot(picked(0, True), outs[pl.ds(count, small)], preferred_element_type=F32)
        + jnp.dot(picked(extra, True), backs[pl.ds(count, small)], preferred_element_type=F32)
    ).astype(BF)

    def put(src, size, first, sem):
        def step(n, carry):
            frm = src.at[pl.ds(pl.multiple_of(n * size, 8), size)]
            to = home.at[pl.ds(pl.multiple_of(n * out_rows + first, 8), size)]
            pltpu.make_async_copy(frm, to, sem).start()
            return carry

        lax.fori_loop(0, nodes, step, 0)

    put(outs, main, 0, sems.at[0])
    put(backs, main, main, sems.at[1])
    put(out_rest, 8, 2 * main, sems.at[2])
    landed(outs.at[pl.ds(0, count)], sems.at[0])
    landed(backs.at[pl.ds(0, count)], sems.at[1])
    landed(out_rest, sems.at[2])


def expert(arrived, pieces, nodes, main, extra, in_rows, x_at, g_at, rest_at, x_rest, g_rest, blocks):
    width = arrived.shape[1]
    rows = nodes * (main + extra)
    hidden = len(pieces) * pieces[0].shape[1]
    out_rows = 2 * main + 8
    body = functools.partial(
        expert_kernel, nodes, main, extra, in_rows, out_rows, x_at, g_at, rest_at, x_rest, g_rest, blocks, len(pieces)
    )
    any_spec = pl.BlockSpec(memory_space=pl.ANY)
    return pl.pallas_call(
        body,
        out_shape=jax.ShapeDtypeStruct((nodes * out_rows, width), BF),
        in_specs=[any_spec] * (1 + len(pieces)),
        out_specs=any_spec,
        scratch_shapes=[
            pltpu.VMEM((rows, width), BF),
            pltpu.VMEM((rows, width), BF),
            pltpu.VMEM((nodes * 8, width), BF),
            pltpu.VMEM((hidden, width), BF),
            pltpu.VMEM((hidden, width), BF),
            pltpu.VMEM((hidden, width), BF),
            pltpu.VMEM((rows, width), BF),
            pltpu.VMEM((rows, width), BF),
            pltpu.VMEM((nodes * 8, width), BF),
            pltpu.SemaphoreType.DMA((6,)),
        ],
        compiler_params=pltpu.CompilerParams(vmem_limit_bytes=60 * 1024 * 1024),
        cost_estimate=pl.CostEstimate(
            flops=12 * rows * hidden * width,
            transcendentals=rows * hidden,
            bytes_accessed=2 * width * (4 * rows + 3 * hidden),
        ),
    )(arrived, *pieces)


def mixed(rows_ref, places, first, values, ids):
    total = 0.0
    for k in range(TOP):
        total = total + jnp.where(places[:, first + k : first + k + 1] == ids, values[:, k : k + 1], 0.0)
    return jnp.dot(total.astype(BF), rows_ref[...], preferred_element_type=F32)


def weight_grads(rows_ref, grads, places, first, ids):
    table = lax.dot_general(grads, rows_ref[...], (((1,), (1,)), ((), ())), preferred_element_type=F32)
    return jnp.concatenate(
        [
            jnp.sum(jnp.where(places[:, first + k : first + k + 1] == ids, table, 0.0), axis=1, keepdims=True)
            for k in range(TOP)
        ],
        axis=1,
    )


def combine_pair_kernel(home, places_ref, values_ref, grads, grads_other, back, own, dw_other, dw_own):
    toks = grads.shape[0]
    ids = lax.broadcasted_iota(jnp.int32, (toks, home.shape[0]), 1)
    places = places_ref[...]
    values, values_other = values_ref[:, :TOP], values_ref[:, TOP:]
    back[:toks] = mixed(home, places, 2 * TOP, values_other, ids).astype(BF)
    back[toks:] = mixed(home, places, 3 * TOP, values_other, ids).astype(BF)
    dw_other[...] = weight_grads(home, grads_other[...], places, 2 * TOP, ids)
    own[:toks] = mixed(home, places, 0, values, ids)
    own[toks:] = mixed(home, places, TOP, values, ids)
    dw_own[...] = weight_grads(home, grads[...], places, 0, ids)


def combine_full_kernel(home, places_ref, values_ref, grads, own, returned, dw_own, dw_back, combined, d_tokens, d_weights):
    toks = grads.shape[0]
    ids = lax.broadcasted_iota(jnp.int32, (toks, home.shape[0]), 1)
    places = places_ref[...]
    values = values_ref[:, :TOP]
    combined[...] = (
        mixed(home, places, 0, values, ids) + own[:toks] + returned[:toks].astype(F32)
    ).astype(BF)
    d_tokens[...] = (
        mixed(home, places, TOP, values, ids) + own[toks:] + returned[toks:].astype(F32)
    ).astype(BF)
    d_weights[...] = weight_grads(home, grads[...], places, 0, ids) + dw_own[...] + dw_back[...]


def combine_pair(home, places, values, grads, other):
    toks, width = grads.shape
    whole = pl.BlockSpec(memory_space=pltpu.VMEM)
    return pl.pallas_call(
        combine_pair_kernel,
        name="combine_pair",
        grid=(1,),
        out_shape=(
            jax.ShapeDtypeStruct((2 * toks, width), BF),
            jax.ShapeDtypeStruct((2 * toks, width), F32),
            jax.ShapeDtypeStruct((toks, TOP), F32),
            jax.ShapeDtypeStruct((toks, TOP), F32),
        ),
        in_specs=[whole] * 4 + [pl.BlockSpec((toks, width), lambda i: (1, 0))],
        out_specs=(whole,) * 4,
        cost_estimate=pl.CostEstimate(
            flops=12 * toks * home.shape[0] * width, transcendentals=0, bytes_accessed=12 * 1024 * 1024
        ),
    )(home, places, values, grads, other)


def combine_full(home, places, values, grads, own, returned, dw_own, dw_back):
    toks, width = grads.shape
    return pl.pallas_call(
        combine_full_kernel,
        name="combine_full",
        out_shape=(
            jax.ShapeDtypeStruct((toks, width), BF),
            jax.ShapeDtypeStruct((toks, width), BF),
            jax.ShapeDtypeStruct((toks, TOP), F32),
        ),
        cost_estimate=pl.CostEstimate(
            flops=6 * toks * home.shape[0] * width, transcendentals=0, bytes_accessed=8 * 1024 * 1024
        ),
    )(home, places, values, grads, own, returned, dw_own, dw_back)


def shards(tokens, route, combine_weights, w_gate, w_up, w_down, grad_out):
    nodes = lax.axis_size("node")
    planes = lax.axis_size("local")
    up = [(i, (i + 1) % planes) for i in range(planes)]
    down = [(i, (i - 1) % planes) for i in range(planes)]
    across = [(i, (i + 2) % planes) for i in range(planes)]

    def send(value, pairs):
        return lax.ppermute(value, "local", pairs)

    def exchange(rows):
        return lax.all_to_all(rows, "node", split_axis=0, concat_axis=0, tiled=True)

    own = jnp.concatenate([tokens, grad_out], axis=0)
    other = send(own, across)
    route_t = route.T
    weight_t = combine_weights.T
    small = send(jnp.concatenate([weight_t, route_t.astype(F32)], axis=0), across)
    weight_other = small[:TOP]
    route_other = small[TOP:].astype(jnp.int32)

    gate_t = jnp.swapaxes(w_gate, 1, 2)
    up_t = jnp.swapaxes(w_up, 1, 2)
    half = gate_t.shape[1] // 2

    def piece(expert, part):
        cut = slice(part * half, (part + 1) * half)
        return jnp.stack([gate_t[expert, cut], up_t[expert, cut], w_down[expert, cut]])

    p0a, p0b, p1a, p1b = piece(0, 0), piece(0, 1), piece(1, 0), piece(1, 1)
    w0 = [p0a, p0b, send(p0a, down), send(p0b, up)]
    below_a, above_b = send(p1a, up), send(p1b, down)
    below_b, above_a = send(p1b, up), send(p1a, down)
    far_a, far_b = send(below_a, up), send(above_b, down)
    w1 = [p1a, p1b, below_a, below_b, above_a, above_b, far_a, far_b]

    slot_own, slot_other = slots_of(route_t), slots_of(route_other)

    def places(route_rows, index, odd, chunk, main, first, rest):
        row = jnp.where(index < main, first + index, rest + index - main)
        return jnp.where(route_rows % 2 == odd, (route_rows // 2) * chunk + row, -1)

    def pair_places(route_rows, index, chunk, first, rest):
        return places(route_rows, index, 0, chunk, 16, first, rest)

    def full_places(chunk, first, rest):
        return places(route_t, slot_own, 1, chunk, 8, first, rest)

    send_rows = jnp.dot(
        jnp.concatenate(
            [
                one_hot_rows(
                    jnp.maximum(
                        pair_places(route_t, slot_own, IN_ROWS, 0, 48),
                        full_places(IN_ROWS, 32, 52),
                    ),
                    nodes * IN_ROWS,
                ),
                one_hot_rows(
                    jnp.maximum(
                        pair_places(route_t, slot_own, IN_ROWS, 16, 50),
                        full_places(IN_ROWS, 40, 53),
                    ),
                    nodes * IN_ROWS,
                ),
                one_hot_rows(
                    pair_places(route_other, slot_other + CAP, IN_ROWS, 0, 48), nodes * IN_ROWS
                ),
                one_hot_rows(
                    pair_places(route_other, slot_other + CAP, IN_ROWS, 16, 50), nodes * IN_ROWS
                ),
            ],
            axis=1,
        ),
        jnp.concatenate([own, other], axis=0),
        preferred_element_type=F32,
    ).astype(BF)

    arrived = exchange(send_rows)
    rows0 = expert(arrived, w0, nodes, 16, 2, IN_ROWS, 0, 16, 48, 0, 2, 1)
    home0 = exchange(rows0)
    rows1 = expert(arrived, w1, nodes, 8, 1, IN_ROWS, 32, 40, 48, 4, 5, 1)
    home1 = exchange(rows1)

    places0 = jnp.concatenate(
        [
            pair_places(route_t, slot_own, OUT0_ROWS, 0, 32),
            pair_places(route_t, slot_own, OUT0_ROWS, 16, 34),
            pair_places(route_other, slot_other + CAP, OUT0_ROWS, 0, 32),
            pair_places(route_other, slot_other + CAP, OUT0_ROWS, 16, 34),
        ],
        axis=0,
    ).T
    places1 = jnp.concatenate(
        [full_places(OUT1_ROWS, 0, 16), full_places(OUT1_ROWS, 8, 17)], axis=0
    ).T
    values = jnp.concatenate([weight_t, weight_other], axis=0).T
    back, kept, dw_other, dw_own = combine_pair(home0, places0, values, grad_out, other)
    returned = send(back, across)
    dw_back = send(dw_other, across)
    return combine_full(home1, places1, values, grad_out, kept, returned, dw_own, dw_back)


def solution(mesh):
    tokens_spec = P(("node", "local"), None)

    return jax.shard_map(
        shards,
        mesh=mesh,
        in_specs=(
            tokens_spec,
            tokens_spec,
            tokens_spec,
            P("node", None, "local"),
            P("node", None, "local"),
            P("node", "local", None),
            tokens_spec,
        ),
        out_specs=(tokens_spec, tokens_spec, tokens_spec),
        check_vma=False,
    )
```

```python
import functools

import jax
import jax.numpy as jnp
from jax import lax
from jax.experimental import pallas as pl
from jax.experimental.pallas import tpu as pltpu
from jax.sharding import PartitionSpec as P

EXPERTS = 64
TOP = 4
BF = jnp.bfloat16
F32 = jnp.float32

OWN_ROWS = 32
OTHER_ROWS = 24
OUT0_ROWS = 40
OUT1_ROWS = 24


def slots_of(route_t):
    toks = route_t.shape[1]
    expert_ids = jnp.arange(EXPERTS, dtype=jnp.int32)[:, None]
    hits = [(route_t[k][None, :] == expert_ids) for k in range(TOP)]
    named = sum(h.astype(BF) for h in hits)
    before = (
        jnp.arange(toks, dtype=jnp.int32)[:, None] < jnp.arange(toks, dtype=jnp.int32)[None, :]
    ).astype(BF)
    earlier = jnp.dot(named, before, preferred_element_type=F32)
    slots = [jnp.sum(jnp.where(h, earlier, 0.0), axis=0) for h in hits]
    return jnp.stack(slots).astype(jnp.int32)


def one_hot_rows(row_t, rows):
    ids = jnp.arange(rows, dtype=jnp.int32)[:, None]
    total = 0
    for k in range(TOP):
        total = total + jnp.where(row_t[k][None, :] == ids, 1.0, 0.0)
    return total.astype(BF)


def landed(dst, sem):
    pltpu.make_async_copy(dst, dst, sem).wait()


def fetch_rows(nodes, src, stride, first, dst, at, sem):
    def step(n, carry):
        frm = src.at[pl.ds(pl.multiple_of(n * stride + first, 8), 8)]
        to = dst.at[pl.ds(pl.multiple_of(at + n * 8, 8), 8)]
        pltpu.make_async_copy(frm, to, sem).start()
        return carry

    lax.fori_loop(0, nodes, step, 0)


def put_rows(nodes, src, at, dst, stride, first, sem):
    def step(n, carry):
        frm = src.at[pl.ds(pl.multiple_of(at + n * 8, 8), 8)]
        to = dst.at[pl.ds(pl.multiple_of(n * stride + first, 8), 8)]
        pltpu.make_async_copy(frm, to, sem).start()
        return carry

    lax.fori_loop(0, nodes, step, 0)


def fetch_weights(pieces, weights, sems, first):
    part = pieces[0].shape[1]
    for j, w in enumerate(weights):
        for i, p in enumerate(pieces):
            pltpu.make_async_copy(p.at[j], w.at[pl.ds(i * part, part)], sems.at[first + j]).start()


def picked(nodes, extra, offset, out_major):
    shape = (nodes * 8, nodes * extra) if out_major else (nodes * extra, nodes * 8)
    compact = lax.broadcasted_iota(jnp.int32, shape, 1 if out_major else 0)
    wide = lax.broadcasted_iota(jnp.int32, shape, 0 if out_major else 1)
    want = (compact // extra) * 8 + offset + compact % extra
    return (want == wide).astype(F32).astype(BF)


def by_hidden(rows, w):
    return lax.dot_general(rows, w, (((1,), (1,)), ((), ())), preferred_element_type=F32)


def by_row(rows, w):
    return jnp.dot(rows, w, preferred_element_type=F32)


def inner(x, g, wg, wu, wd):
    gate = by_hidden(x, wg)
    upper = by_hidden(x, wu)
    d_hidden = by_hidden(g, wd)
    s = jax.nn.sigmoid(gate)
    act = gate * s
    hidden = (act * upper).astype(BF)
    d_gate = (d_hidden * upper * s * (1.0 + gate * (1.0 - s))).astype(BF)
    d_up = (d_hidden * act).astype(BF)
    return hidden, d_gate, d_up


def expert_pair_kernel(nodes, n_pieces, *refs):
    arrived, arrived_other, pieces, home = refs[0], refs[1], refs[2 : 2 + n_pieces], refs[2 + n_pieces]
    xs, gs, rest, wg, wu, wd, outs, backs, out_rest, sems = refs[3 + n_pieces :]
    main, small = nodes * 16, nodes * 2
    fetch_rows(nodes, arrived, OWN_ROWS, 0, xs, 0, sems.at[0])
    fetch_rows(nodes, arrived_other, OTHER_ROWS, 0, xs, nodes * 8, sems.at[0])
    fetch_rows(nodes, arrived_other, OTHER_ROWS, 16, rest, 0, sems.at[1])
    fetch_weights(pieces, (wg, wu, wd), sems, 3)
    fetch_rows(nodes, arrived, OWN_ROWS, 8, gs, 0, sems.at[2])
    fetch_rows(nodes, arrived_other, OTHER_ROWS, 8, gs, nodes * 8, sems.at[2])
    landed(rest, sems.at[1])
    xs[pl.ds(main, small)] = by_row(picked(nodes, 2, 0, False), rest[...]).astype(BF)
    gs[pl.ds(main, small)] = by_row(picked(nodes, 2, 2, False), rest[...]).astype(BF)
    landed(xs.at[pl.ds(0, main)], sems.at[0])
    landed(wg, sems.at[3])
    landed(wu, sems.at[4])
    landed(gs.at[pl.ds(0, main)], sems.at[2])
    landed(wd, sems.at[5])
    size = (main + small) // 2

    def block(b, carry):
        at = pl.ds(pl.multiple_of(b * size, 16), size)
        hidden, d_gate, d_up = inner(xs[at], gs[at], wg[...], wu[...], wd[...])
        outs[at] = by_row(hidden, wd[...]).astype(BF)
        backs[at] = (by_row(d_gate, wg[...]) + by_row(d_up, wu[...])).astype(BF)
        return carry

    lax.fori_loop(0, 2, block, 0)
    put_rows(nodes, outs, 0, home, OUT0_ROWS, 0, sems.at[0])
    put_rows(nodes, outs, nodes * 8, home, OUT0_ROWS, 8, sems.at[0])
    put_rows(nodes, backs, 0, home, OUT0_ROWS, 16, sems.at[1])
    put_rows(nodes, backs, nodes * 8, home, OUT0_ROWS, 24, sems.at[1])
    out_rest[...] = (
        by_row(picked(nodes, 2, 0, True), outs[pl.ds(main, small)])
        + by_row(picked(nodes, 2, 2, True), backs[pl.ds(main, small)])
    ).astype(BF)
    put_rows(nodes, out_rest, 0, home, OUT0_ROWS, 32, sems.at[2])
    landed(outs.at[pl.ds(0, main)], sems.at[0])
    landed(backs.at[pl.ds(0, main)], sems.at[1])
    landed(out_rest, sems.at[2])


def expert_near_kernel(nodes, n_pieces, *refs):
    arrived, arrived_other, pieces = refs[0], refs[1], refs[2 : 2 + n_pieces]
    out_part, back_part, xs, gs = refs[2 + n_pieces : 6 + n_pieces]
    rest, wg, wu, wd, sems = refs[6 + n_pieces :]
    main, small = nodes * 8, nodes
    fetch_rows(nodes, arrived, OWN_ROWS, 16, xs, 0, sems.at[0])
    fetch_rows(nodes, arrived, OWN_ROWS, 24, gs, 0, sems.at[2])
    fetch_rows(nodes, arrived_other, OTHER_ROWS, 16, rest, 0, sems.at[1])
    fetch_weights(pieces, (wg, wu, wd), sems, 3)
    landed(rest, sems.at[1])
    landed(xs.at[pl.ds(0, main)], sems.at[0])
    landed(gs.at[pl.ds(0, main)], sems.at[2])
    xs[pl.ds(main, small)] = by_row(picked(nodes, 1, 4, False), rest[...]).astype(BF)
    gs[pl.ds(main, small)] = by_row(picked(nodes, 1, 5, False), rest[...]).astype(BF)
    landed(wg, sems.at[3])
    landed(wu, sems.at[4])
    landed(wd, sems.at[5])
    hidden, d_gate, d_up = inner(xs[...], gs[...], wg[...], wu[...], wd[...])
    out_part[...] = by_row(hidden, wd[...])
    back_part[...] = by_row(d_gate, wg[...]) + by_row(d_up, wu[...])


def expert_far_kernel(nodes, n_pieces, *refs):
    xs, gs, out_part, back_part = refs[:4]
    pieces, home = refs[4 : 4 + n_pieces], refs[4 + n_pieces]
    wg, wu, wd, outs, backs, out_rest, sems = refs[5 + n_pieces :]
    main, small = nodes * 8, nodes
    fetch_weights(pieces, (wg, wu, wd), sems, 3)
    for j, w in enumerate((wg, wu, wd)):
        landed(w, sems.at[3 + j])
    hidden, d_gate, d_up = inner(xs[...], gs[...], wg[...], wu[...], wd[...])
    outs[...] = (by_row(hidden, wd[...]) + out_part[...]).astype(BF)
    put_rows(nodes, outs, 0, home, OUT1_ROWS, 0, sems.at[0])
    backs[...] = (by_row(d_gate, wg[...]) + by_row(d_up, wu[...]) + back_part[...]).astype(BF)
    put_rows(nodes, backs, 0, home, OUT1_ROWS, 8, sems.at[1])
    out_rest[...] = (
        by_row(picked(nodes, 1, 0, True), outs[pl.ds(main, small)])
        + by_row(picked(nodes, 1, 1, True), backs[pl.ds(main, small)])
    ).astype(BF)
    put_rows(nodes, out_rest, 0, home, OUT1_ROWS, 16, sems.at[2])
    landed(outs.at[pl.ds(0, main)], sems.at[0])
    landed(backs.at[pl.ds(0, main)], sems.at[1])
    landed(out_rest, sems.at[2])


ANY = pl.BlockSpec(memory_space=pl.ANY)
WHOLE = pl.BlockSpec(memory_space=pltpu.VMEM)
PARAMS = pltpu.CompilerParams(vmem_limit_bytes=60 * 1024 * 1024)


def expert_cost(rows, hidden, width):
    return pl.CostEstimate(
        flops=12 * rows * hidden * width,
        transcendentals=rows * hidden,
        bytes_accessed=2 * width * (4 * rows + 3 * hidden),
    )


def expert_pair(arrived, arrived_other, pieces, nodes):
    width = arrived.shape[1]
    rows, hidden = nodes * 18, len(pieces) * pieces[0].shape[1]
    scratch = [(rows, width), (rows, width), (nodes * 8, width)] + [(hidden, width)] * 3
    scratch += [(rows, width), (rows, width), (nodes * 8, width)]
    return pl.pallas_call(
        functools.partial(expert_pair_kernel, nodes, len(pieces)),
        name="expert_pair",
        out_shape=jax.ShapeDtypeStruct((nodes * OUT0_ROWS, width), BF),
        in_specs=[ANY] * (2 + len(pieces)),
        out_specs=ANY,
        scratch_shapes=[pltpu.VMEM(s, BF) for s in scratch] + [pltpu.SemaphoreType.DMA((6,))],
        compiler_params=PARAMS,
        cost_estimate=expert_cost(rows, hidden, width),
    )(arrived, arrived_other, *pieces)


def expert_near(arrived, arrived_other, pieces, nodes):
    width = arrived.shape[1]
    rows, hidden = nodes * 9, len(pieces) * pieces[0].shape[1]
    scratch = [(nodes * 8, width)] + [(hidden, width)] * 3
    return pl.pallas_call(
        functools.partial(expert_near_kernel, nodes, len(pieces)),
        name="expert_near",
        out_shape=tuple(jax.ShapeDtypeStruct((rows, width), t) for t in (F32, F32, BF, BF)),
        in_specs=[ANY] * (2 + len(pieces)),
        out_specs=(WHOLE,) * 4,
        scratch_shapes=[pltpu.VMEM(s, BF) for s in scratch] + [pltpu.SemaphoreType.DMA((6,))],
        compiler_params=PARAMS,
        cost_estimate=expert_cost(rows, hidden, width),
    )(arrived, arrived_other, *pieces)


def expert_far(near, pieces, nodes):
    out_part, back_part, xs, gs = near
    rows, width = xs.shape
    hidden = len(pieces) * pieces[0].shape[1]
    scratch = [(hidden, width)] * 3 + [(rows, width), (rows, width), (nodes * 8, width)]
    return pl.pallas_call(
        functools.partial(expert_far_kernel, nodes, len(pieces)),
        name="expert_far",
        out_shape=jax.ShapeDtypeStruct((nodes * OUT1_ROWS, width), BF),
        in_specs=[WHOLE] * 4 + [ANY] * len(pieces),
        out_specs=ANY,
        scratch_shapes=[pltpu.VMEM(s, BF) for s in scratch] + [pltpu.SemaphoreType.DMA((6,))],
        compiler_params=PARAMS,
        cost_estimate=expert_cost(rows, hidden, width),
    )(xs, gs, out_part, back_part, *pieces)


def mixed(rows_ref, places, first, values, ids):
    total = 0.0
    for k in range(TOP):
        total = total + jnp.where(places[:, first + k : first + k + 1] == ids, values[:, k : k + 1], 0.0)
    return jnp.dot(total.astype(BF), rows_ref[...], preferred_element_type=F32)


def weight_grads(rows_ref, grads, places, first, ids):
    table = lax.dot_general(grads, rows_ref[...], (((1,), (1,)), ((), ())), preferred_element_type=F32)
    return jnp.concatenate(
        [
            jnp.sum(jnp.where(places[:, first + k : first + k + 1] == ids, table, 0.0), axis=1, keepdims=True)
            for k in range(TOP)
        ],
        axis=1,
    )


def combine_pair_kernel(home, places_ref, values_ref, grads, grads_other, back, own, dw_other, dw_own):
    toks = grads.shape[0]
    ids = lax.broadcasted_iota(jnp.int32, (toks, home.shape[0]), 1)
    places = places_ref[...]
    values, values_other = values_ref[:, :TOP], values_ref[:, TOP:]
    back[:toks] = mixed(home, places, 2 * TOP, values_other, ids).astype(BF)
    back[toks:] = mixed(home, places, 3 * TOP, values_other, ids).astype(BF)
    dw_other[...] = weight_grads(home, grads_other[...], places, 2 * TOP, ids)
    own[:toks] = mixed(home, places, 0, values, ids)
    own[toks:] = mixed(home, places, TOP, values, ids)
    dw_own[...] = weight_grads(home, grads[...], places, 0, ids)


def combine_full_kernel(home, places_ref, values_ref, grads, own, returned, dw_own, dw_back, combined, d_tokens, d_weights):
    toks = grads.shape[0]
    ids = lax.broadcasted_iota(jnp.int32, (toks, home.shape[0]), 1)
    places = places_ref[...]
    values = values_ref[:, :TOP]
    combined[...] = (
        mixed(home, places, 0, values, ids) + own[:toks] + returned[:toks].astype(F32)
    ).astype(BF)
    d_tokens[...] = (
        mixed(home, places, TOP, values, ids) + own[toks:] + returned[toks:].astype(F32)
    ).astype(BF)
    d_weights[...] = weight_grads(home, grads[...], places, 0, ids) + dw_own[...] + dw_back[...]


def combine_pair(home, places, values, grads, other):
    toks, width = grads.shape
    whole = pl.BlockSpec(memory_space=pltpu.VMEM)
    return pl.pallas_call(
        combine_pair_kernel,
        name="combine_pair",
        grid=(1,),
        out_shape=(
            jax.ShapeDtypeStruct((2 * toks, width), BF),
            jax.ShapeDtypeStruct((2 * toks, width), F32),
            jax.ShapeDtypeStruct((toks, TOP), F32),
            jax.ShapeDtypeStruct((toks, TOP), F32),
        ),
        in_specs=[whole] * 4 + [pl.BlockSpec((toks, width), lambda i: (1, 0))],
        out_specs=(whole,) * 4,
        cost_estimate=pl.CostEstimate(
            flops=12 * toks * home.shape[0] * width, transcendentals=0, bytes_accessed=12 * 1024 * 1024
        ),
    )(home, places, values, grads, other)


def combine_full(home, places, values, grads, own, returned, dw_own, dw_back):
    toks, width = grads.shape
    return pl.pallas_call(
        combine_full_kernel,
        name="combine_full",
        out_shape=(
            jax.ShapeDtypeStruct((toks, width), BF),
            jax.ShapeDtypeStruct((toks, width), BF),
            jax.ShapeDtypeStruct((toks, TOP), F32),
        ),
        cost_estimate=pl.CostEstimate(
            flops=6 * toks * home.shape[0] * width, transcendentals=0, bytes_accessed=8 * 1024 * 1024
        ),
    )(home, places, values, grads, own, returned, dw_own, dw_back)


def shards(tokens, route, combine_weights, w_gate, w_up, w_down, grad_out):
    nodes = lax.axis_size("node")
    planes = lax.axis_size("local")
    up = [(i, (i + 1) % planes) for i in range(planes)]
    down = [(i, (i - 1) % planes) for i in range(planes)]
    across = [(i, (i + 2) % planes) for i in range(planes)]

    def send(value, pairs):
        return lax.ppermute(value, "local", pairs)

    def exchange(rows):
        return lax.all_to_all(rows, "node", split_axis=0, concat_axis=0, tiled=True)

    own = jnp.concatenate([tokens, grad_out], axis=0)
    other = send(own, across)
    route_t = route.T
    weight_t = combine_weights.T
    small = send(jnp.concatenate([weight_t, route_t.astype(F32)], axis=0), across)
    weight_other = small[:TOP]
    route_other = small[TOP:].astype(jnp.int32)

    gate_t = jnp.swapaxes(w_gate, 1, 2)
    up_t = jnp.swapaxes(w_up, 1, 2)
    half = gate_t.shape[1] // 2

    def piece(expert, part):
        cut = slice(part * half, (part + 1) * half)
        return jnp.stack([gate_t[expert, cut], up_t[expert, cut], w_down[expert, cut]])

    p0a, p0b, p1a, p1b = piece(0, 0), piece(0, 1), piece(1, 0), piece(1, 1)
    w0 = [p0a, p0b, send(p0a, down), send(p0b, up)]
    below_a, above_b = send(p1a, up), send(p1b, down)
    below_b, above_a = send(p1b, up), send(p1a, down)
    far_a, far_b = send(below_a, up), send(above_b, down)
    w1 = [p1a, p1b, below_a, below_b, above_a, above_b, far_a, far_b]

    slot_own, slot_other = slots_of(route_t), slots_of(route_other)

    def places(route_rows, row, keep):
        chunk, index = row
        return jnp.where(keep, (route_rows // 2) * chunk + index, -1)

    own_even, other_even = route_t % 2 == 0, route_other % 2 == 0
    own_main, other_main = slot_own < 8, slot_other < 8

    def own_place(first_even, first_odd):
        index = jnp.where(own_even, first_even, first_odd) + slot_own
        return places(route_t, (OWN_ROWS, index), own_main)

    def rest_place(even, odd):
        return places(route_t, (OTHER_ROWS, jnp.where(own_even, even, odd)), ~own_main)

    def other_place(main, rest, chunk):
        index = jnp.where(other_main, main + slot_other, rest)
        return places(route_other, (chunk, index), other_even)

    own_rows = jnp.dot(
        jnp.concatenate(
            [
                one_hot_rows(own_place(0, 16), nodes * OWN_ROWS),
                one_hot_rows(own_place(8, 24), nodes * OWN_ROWS),
            ],
            axis=1,
        ),
        own,
        preferred_element_type=F32,
    ).astype(BF)
    arrived = exchange(own_rows)
    other_rows = jnp.dot(
        jnp.concatenate(
            [
                one_hot_rows(rest_place(16, 20), nodes * OTHER_ROWS),
                one_hot_rows(rest_place(18, 21), nodes * OTHER_ROWS),
                one_hot_rows(other_place(0, 17, OTHER_ROWS), nodes * OTHER_ROWS),
                one_hot_rows(other_place(8, 19, OTHER_ROWS), nodes * OTHER_ROWS),
            ],
            axis=1,
        ),
        jnp.concatenate([own, other], axis=0),
        preferred_element_type=F32,
    ).astype(BF)
    arrived_other = exchange(other_rows)

    rows0 = expert_pair(arrived, arrived_other, w0, nodes)
    home0 = exchange(rows0)
    near = expert_near(arrived, arrived_other, w1[:6], nodes)
    rows1 = expert_far(near, w1[6:], nodes)
    home1 = exchange(rows1)

    def home_place(main, rest):
        index = jnp.where(own_main, main + slot_own, rest)
        return places(route_t, (OUT0_ROWS, index), own_even)

    def full_place(main, rest):
        index = jnp.where(own_main, main + slot_own, rest)
        return places(route_t, (OUT1_ROWS, index), ~own_even)

    places0 = jnp.concatenate(
        [
            home_place(0, 32),
            home_place(16, 34),
            other_place(8, 33, OUT0_ROWS),
            other_place(24, 35, OUT0_ROWS),
        ],
        axis=0,
    ).T
    places1 = jnp.concatenate([full_place(0, 16), full_place(8, 17)], axis=0).T
    values = jnp.concatenate([weight_t, weight_other], axis=0).T
    back, kept, dw_other, dw_own = combine_pair(home0, places0, values, grad_out, other)
    returned = send(back, across)
    dw_back = send(dw_other, across)
    return combine_full(home1, places1, values, grad_out, kept, returned, dw_own, dw_back)


def solution(mesh):
    tokens_spec = P(("node", "local"), None)

    return jax.shard_map(
        shards,
        mesh=mesh,
        in_specs=(
            tokens_spec,
            tokens_spec,
            tokens_spec,
            P("node", None, "local"),
            P("node", None, "local"),
            P("node", "local", None),
            tokens_spec,
        ),
        out_specs=(tokens_spec, tokens_spec, tokens_spec),
        check_vma=False,
    )
```

```python
import functools

import jax
import jax.numpy as jnp
from jax import lax
from jax.experimental import pallas as pl
from jax.experimental.pallas import tpu as pltpu
from jax.sharding import PartitionSpec as P

EXPERTS = 64
TOP = 4
BF = jnp.bfloat16
F32 = jnp.float32

OWN_ROWS = 32
OTHER_ROWS = 24
OUT0_ROWS = 40
OUT1_ROWS = 24


def slots_of(route_t):
    toks = route_t.shape[1]
    expert_ids = lax.broadcasted_iota(jnp.int32, (EXPERTS, toks), 0)
    hits = [(route_t[k : k + 1] == expert_ids) for k in range(TOP)]
    named = sum(jnp.where(h, 1.0, 0.0) for h in hits).astype(BF)
    from_ids = lax.broadcasted_iota(jnp.int32, (toks, toks), 0)
    to_ids = lax.broadcasted_iota(jnp.int32, (toks, toks), 1)
    before = jnp.where(from_ids < to_ids, 1.0, 0.0).astype(BF)
    earlier = jnp.dot(named, before, preferred_element_type=F32)
    slots = [jnp.sum(jnp.where(h, earlier, 0.0), axis=0, keepdims=True) for h in hits]
    return jnp.concatenate(slots, axis=0).astype(jnp.int32)


def dispatch_rows(pairs, block, first):
    total = None
    for places, values in pairs:
        ids = lax.broadcasted_iota(jnp.int32, (block, places.shape[1]), 0) + first
        hot = jnp.zeros(ids.shape, F32)
        for k in range(TOP):
            hot = hot + jnp.where(places[k : k + 1] == ids, 1.0, 0.0)
        term = jnp.dot(hot.astype(BF), values, preferred_element_type=F32)
        total = term if total is None else total + term
    return total.astype(BF)


def dispatch_own_kernel(route_ref, tokens, grads, rows):
    block = rows.shape[0]
    first = pl.program_id(0) * block
    route = route_ref[...]
    slot = slots_of(route)
    base = (route // 2) * OWN_ROWS + (route % 2) * 16 + slot
    kept = slot < 8
    x_place, g_place = jnp.where(kept, base, -1), jnp.where(kept, base + 8, -1)
    rows[...] = dispatch_rows([(x_place, tokens[...]), (g_place, grads[...])], block, first)


def dispatch_other_kernel(route_ref, route_other_ref, tokens, grads, tokens_other, grads_other, rows):
    block = rows.shape[0]
    first = pl.program_id(0) * block
    route = route_ref[...]
    odd = route % 2
    ninth = slots_of(route) == 8
    base = (route // 2) * OTHER_ROWS
    x_place = jnp.where(ninth, base + 16 + 4 * odd, -1)
    g_place = jnp.where(ninth, base + 18 + 3 * odd, -1)
    route = route_other_ref[...]
    even = route % 2 == 0
    slot = slots_of(route)
    base = (route // 2) * OTHER_ROWS
    x_far = jnp.where(even, base + jnp.where(slot < 8, slot, 17), -1)
    g_far = jnp.where(even, base + jnp.where(slot < 8, slot + 8, 19), -1)
    rows[...] = dispatch_rows(
        [(x_place, tokens[...]), (g_place, grads[...]), (x_far, tokens_other[...]), (g_far, grads_other[...])],
        block,
        first,
    )


def dispatch(kernel, rows, *args):
    width = args[-1].shape[1]
    steps = 4

    def whole(x):
        return pl.BlockSpec(x.shape, lambda i: (0, 0))

    return pl.pallas_call(
        kernel,
        grid=(steps,),
        out_shape=jax.ShapeDtypeStruct((rows, width), BF),
        in_specs=[whole(x) for x in args],
        out_specs=pl.BlockSpec((rows // steps, width), lambda i: (i, 0)),
        cost_estimate=pl.CostEstimate(
            flops=4 * rows * 128 * width, transcendentals=0, bytes_accessed=4 * rows * width
        ),
    )(*args)


def landed(dst, sem):
    pltpu.make_async_copy(dst, dst, sem).wait()


def fetch_rows(nodes, src, stride, first, dst, at, sem):
    def step(n, carry):
        frm = src.at[pl.ds(pl.multiple_of(n * stride + first, 8), 8)]
        to = dst.at[pl.ds(pl.multiple_of(at + n * 8, 8), 8)]
        pltpu.make_async_copy(frm, to, sem).start()
        return carry

    lax.fori_loop(0, nodes, step, 0)


def put_rows(nodes, src, at, dst, stride, first, sem):
    def step(n, carry):
        frm = src.at[pl.ds(pl.multiple_of(at + n * 8, 8), 8)]
        to = dst.at[pl.ds(pl.multiple_of(n * stride + first, 8), 8)]
        pltpu.make_async_copy(frm, to, sem).start()
        return carry

    lax.fori_loop(0, nodes, step, 0)


def fetch_weights(pieces, weights, sems, first):
    part = pieces[0].shape[1]
    for j, w in enumerate(weights):
        for i, p in enumerate(pieces):
            pltpu.make_async_copy(p.at[j], w.at[pl.ds(i * part, part)], sems.at[first + j]).start()


def picked(nodes, extra, offset, out_major):
    shape = (nodes * 8, nodes * extra) if out_major else (nodes * extra, nodes * 8)
    compact = lax.broadcasted_iota(jnp.int32, shape, 1 if out_major else 0)
    wide = lax.broadcasted_iota(jnp.int32, shape, 0 if out_major else 1)
    want = (compact // extra) * 8 + offset + compact % extra
    return (want == wide).astype(F32).astype(BF)


def by_hidden(rows, w):
    return lax.dot_general(rows, w, (((1,), (1,)), ((), ())), preferred_element_type=F32)


def by_row(rows, w):
    return jnp.dot(rows, w, preferred_element_type=F32)


def inner(x, g, wg, wu, wd):
    gate = by_hidden(x, wg)
    upper = by_hidden(x, wu)
    d_hidden = by_hidden(g, wd)
    s = jax.nn.sigmoid(gate)
    act = gate * s
    hidden = (act * upper).astype(BF)
    d_gate = (d_hidden * upper * s * (1.0 + gate * (1.0 - s))).astype(BF)
    d_up = (d_hidden * act).astype(BF)
    return hidden, d_gate, d_up


def expert_pair_kernel(nodes, n_pieces, *refs):
    arrived, arrived_other, pieces, home = refs[0], refs[1], refs[2 : 2 + n_pieces], refs[2 + n_pieces]
    xs, gs, rest, wg, wu, wd, outs, backs, out_rest, sems = refs[3 + n_pieces :]
    main, small = nodes * 16, nodes * 2
    fetch_rows(nodes, arrived, OWN_ROWS, 0, xs, 0, sems.at[0])
    fetch_rows(nodes, arrived_other, OTHER_ROWS, 0, xs, nodes * 8, sems.at[0])
    fetch_rows(nodes, arrived_other, OTHER_ROWS, 16, rest, 0, sems.at[1])
    fetch_weights(pieces, (wg, wu, wd), sems, 3)
    fetch_rows(nodes, arrived, OWN_ROWS, 8, gs, 0, sems.at[2])
    fetch_rows(nodes, arrived_other, OTHER_ROWS, 8, gs, nodes * 8, sems.at[2])
    landed(rest, sems.at[1])
    xs[pl.ds(main, small)] = by_row(picked(nodes, 2, 0, False), rest[...]).astype(BF)
    gs[pl.ds(main, small)] = by_row(picked(nodes, 2, 2, False), rest[...]).astype(BF)
    landed(xs.at[pl.ds(0, main)], sems.at[0])
    landed(wg, sems.at[3])
    landed(wu, sems.at[4])
    landed(gs.at[pl.ds(0, main)], sems.at[2])
    landed(wd, sems.at[5])
    size = (main + small) // 2

    def block(b, carry):
        at = pl.ds(pl.multiple_of(b * size, 16), size)
        hidden, d_gate, d_up = inner(xs[at], gs[at], wg[...], wu[...], wd[...])
        outs[at] = by_row(hidden, wd[...]).astype(BF)
        backs[at] = (by_row(d_gate, wg[...]) + by_row(d_up, wu[...])).astype(BF)
        return carry

    lax.fori_loop(0, 2, block, 0)
    put_rows(nodes, outs, 0, home, OUT0_ROWS, 0, sems.at[0])
    put_rows(nodes, outs, nodes * 8, home, OUT0_ROWS, 8, sems.at[0])
    put_rows(nodes, backs, 0, home, OUT0_ROWS, 16, sems.at[1])
    put_rows(nodes, backs, nodes * 8, home, OUT0_ROWS, 24, sems.at[1])
    out_rest[...] = (
        by_row(picked(nodes, 2, 0, True), outs[pl.ds(main, small)])
        + by_row(picked(nodes, 2, 2, True), backs[pl.ds(main, small)])
    ).astype(BF)
    put_rows(nodes, out_rest, 0, home, OUT0_ROWS, 32, sems.at[2])
    landed(outs.at[pl.ds(0, main)], sems.at[0])
    landed(backs.at[pl.ds(0, main)], sems.at[1])
    landed(out_rest, sems.at[2])


def expert_near_kernel(nodes, n_pieces, *refs):
    arrived, arrived_other, pieces = refs[0], refs[1], refs[2 : 2 + n_pieces]
    out_part, back_part, xs, gs = refs[2 + n_pieces : 6 + n_pieces]
    rest, wg, wu, wd, sems = refs[6 + n_pieces :]
    main, small = nodes * 8, nodes
    fetch_rows(nodes, arrived, OWN_ROWS, 16, xs, 0, sems.at[0])
    fetch_rows(nodes, arrived, OWN_ROWS, 24, gs, 0, sems.at[2])
    fetch_rows(nodes, arrived_other, OTHER_ROWS, 16, rest, 0, sems.at[1])
    fetch_weights(pieces, (wg, wu, wd), sems, 3)
    landed(rest, sems.at[1])
    landed(xs.at[pl.ds(0, main)], sems.at[0])
    landed(gs.at[pl.ds(0, main)], sems.at[2])
    xs[pl.ds(main, small)] = by_row(picked(nodes, 1, 4, False), rest[...]).astype(BF)
    gs[pl.ds(main, small)] = by_row(picked(nodes, 1, 5, False), rest[...]).astype(BF)
    landed(wg, sems.at[3])
    landed(wu, sems.at[4])
    landed(wd, sems.at[5])
    size = (main + small) // 2

    def block(b, carry):
        at = pl.ds(pl.multiple_of(b * size, 16), size)
        hidden, d_gate, d_up = inner(xs[at], gs[at], wg[...], wu[...], wd[...])
        out_part[at] = by_row(hidden, wd[...])
        back_part[at] = by_row(d_gate, wg[...]) + by_row(d_up, wu[...])
        return carry

    lax.fori_loop(0, 2, block, 0)


def expert_far_kernel(nodes, n_pieces, *refs):
    near, pieces, home = refs[:4], refs[4 : 4 + n_pieces], refs[4 + n_pieces]
    xs, gs, out_part, back_part, wg, wu, wd, outs, backs, out_rest, sems = refs[5 + n_pieces :]
    main, small = nodes * 8, nodes
    pltpu.make_async_copy(near[0], xs, sems.at[6]).start()
    fetch_weights(pieces, (wg, wu, wd), sems, 3)
    pltpu.make_async_copy(near[1], gs, sems.at[7]).start()
    pltpu.make_async_copy(near[2], out_part, sems.at[8]).start()
    pltpu.make_async_copy(near[3], back_part, sems.at[9]).start()
    landed(xs, sems.at[6])
    landed(wg, sems.at[3])
    landed(wu, sems.at[4])
    landed(wd, sems.at[5])
    landed(gs, sems.at[7])
    hidden, d_gate, d_up = inner(xs[...], gs[...], wg[...], wu[...], wd[...])
    landed(out_part, sems.at[8])
    outs[...] = (by_row(hidden, wd[...]) + out_part[...]).astype(BF)
    put_rows(nodes, outs, 0, home, OUT1_ROWS, 0, sems.at[0])
    landed(back_part, sems.at[9])
    backs[...] = (by_row(d_gate, wg[...]) + by_row(d_up, wu[...]) + back_part[...]).astype(BF)
    put_rows(nodes, backs, 0, home, OUT1_ROWS, 8, sems.at[1])
    out_rest[...] = (
        by_row(picked(nodes, 1, 0, True), outs[pl.ds(main, small)])
        + by_row(picked(nodes, 1, 1, True), backs[pl.ds(main, small)])
    ).astype(BF)
    put_rows(nodes, out_rest, 0, home, OUT1_ROWS, 16, sems.at[2])
    landed(outs.at[pl.ds(0, main)], sems.at[0])
    landed(backs.at[pl.ds(0, main)], sems.at[1])
    landed(out_rest, sems.at[2])


ANY = pl.BlockSpec(memory_space=pltpu.HBM)
WHOLE = pl.BlockSpec(memory_space=pltpu.VMEM)
PARAMS = pltpu.CompilerParams(vmem_limit_bytes=60 * 1024 * 1024)


def expert_cost(rows, hidden, width):
    return pl.CostEstimate(
        flops=12 * rows * hidden * width,
        transcendentals=rows * hidden,
        bytes_accessed=2 * width * (4 * rows + 3 * hidden),
    )


def expert_pair(arrived, arrived_other, pieces, nodes):
    width = arrived.shape[1]
    rows, hidden = nodes * 18, len(pieces) * pieces[0].shape[1]
    scratch = [(rows, width), (rows, width), (nodes * 8, width)] + [(hidden, width)] * 3
    scratch += [(rows, width), (rows, width), (nodes * 8, width)]
    return pl.pallas_call(
        functools.partial(expert_pair_kernel, nodes, len(pieces)),
        name="expert_pair",
        out_shape=jax.ShapeDtypeStruct((nodes * OUT0_ROWS, width), BF),
        in_specs=[ANY] * (2 + len(pieces)),
        out_specs=ANY,
        scratch_shapes=[pltpu.VMEM(s, BF) for s in scratch] + [pltpu.SemaphoreType.DMA((6,))],
        compiler_params=PARAMS,
        cost_estimate=expert_cost(rows, hidden, width),
    )(arrived, arrived_other, *pieces)


def expert_near(arrived, arrived_other, pieces, nodes):
    width = arrived.shape[1]
    rows, hidden = nodes * 9, len(pieces) * pieces[0].shape[1]
    scratch = [(nodes * 8, width)] + [(hidden, width)] * 3
    return pl.pallas_call(
        functools.partial(expert_near_kernel, nodes, len(pieces)),
        name="expert_near",
        out_shape=tuple(jax.ShapeDtypeStruct((rows, width), t) for t in (F32, F32, BF, BF)),
        in_specs=[ANY] * (2 + len(pieces)),
        out_specs=(WHOLE,) * 4,
        scratch_shapes=[pltpu.VMEM(s, BF) for s in scratch] + [pltpu.SemaphoreType.DMA((6,))],
        compiler_params=PARAMS,
        cost_estimate=expert_cost(rows, hidden, width),
    )(arrived, arrived_other, *pieces)


def expert_far(near, pieces, nodes):
    out_part, back_part, xs, gs = near
    rows, width = xs.shape
    hidden = len(pieces) * pieces[0].shape[1]
    scratch = [((rows, width), BF)] * 2 + [((rows, width), F32)] * 2 + [((hidden, width), BF)] * 3
    scratch += [((rows, width), BF)] * 2 + [((nodes * 8, width), BF)]
    return pl.pallas_call(
        functools.partial(expert_far_kernel, nodes, len(pieces)),
        name="expert_far",
        out_shape=jax.ShapeDtypeStruct((nodes * OUT1_ROWS, width), BF),
        in_specs=[ANY] * (4 + len(pieces)),
        out_specs=ANY,
        scratch_shapes=[pltpu.VMEM(s, t) for s, t in scratch] + [pltpu.SemaphoreType.DMA((10,))],
        compiler_params=PARAMS,
        cost_estimate=expert_cost(rows, hidden, width),
    )(xs, gs, out_part, back_part, *pieces)


def mixed(rows, places, values):
    ids = lax.broadcasted_iota(jnp.int32, (places.shape[0], rows.shape[0]), 1)
    total = jnp.zeros(ids.shape, F32)
    for k in range(TOP):
        total = total + jnp.where(places[:, k : k + 1] == ids, values[:, k : k + 1], 0.0)
    return jnp.dot(total.astype(BF), rows, preferred_element_type=F32)


def weight_grads(rows, grads, places):
    table = lax.dot_general(grads, rows, (((1,), (1,)), ((), ())), preferred_element_type=F32)
    ids = lax.broadcasted_iota(jnp.int32, table.shape, 1)
    lane = lax.broadcasted_iota(jnp.int32, (table.shape[0], 128), 1)
    result = jnp.zeros(lane.shape, F32)
    for k in range(TOP):
        column = jnp.sum(jnp.where(places[:, k : k + 1] == ids, table, 0.0), axis=1, keepdims=True)
        result = result + jnp.where(lane == k, column, 0.0)
    return result


def combine_pair_kernel(home, places_ref, values_ref, grads, grads_other, back, own, dw_other, dw_own):
    toks = grads.shape[0]
    rows = home[...]
    total = mixed(rows, places_ref[...], values_ref[...])
    back[...] = total[: 2 * toks].astype(BF)
    own[...] = total[2 * toks :]
    dw_other[...] = jnp.transpose(weight_grads(rows, grads_other[...], places_ref[:toks]))[:8]
    dw_own[...] = jnp.transpose(weight_grads(rows, grads[...], places_ref[2 * toks : 3 * toks]))[:8]


def combine_full_kernel(home, places_ref, values_ref, grads, own, returned, dw_own, dw_back, combined, d_tokens, d_weights):
    toks = grads.shape[0]
    rows = home[...]
    total = mixed(rows, places_ref[...], values_ref[...]) + own[...] + returned[...].astype(F32)
    combined[...] = total[:toks].astype(BF)
    d_tokens[...] = total[toks:].astype(BF)
    dw = jnp.transpose(weight_grads(rows, grads[...], places_ref[:toks]))[:8] + dw_own[...] + dw_back[...]
    d_weights[...] = dw[:TOP]


def combine_pair(home, places, values, grads, grads_other):
    toks, width = grads.shape
    return pl.pallas_call(
        combine_pair_kernel,
        name="combine_pair",
        out_shape=(
            jax.ShapeDtypeStruct((2 * toks, width), BF),
            jax.ShapeDtypeStruct((2 * toks, width), F32),
            jax.ShapeDtypeStruct((8, toks), F32),
            jax.ShapeDtypeStruct((8, toks), F32),
        ),
        cost_estimate=pl.CostEstimate(
            flops=12 * toks * home.shape[0] * width, transcendentals=0, bytes_accessed=12 * 1024 * 1024
        ),
    )(home, places, values, grads, grads_other)


def combine_full(home, places, values, grads, own, returned, dw_own, dw_back):
    toks, width = grads.shape
    return pl.pallas_call(
        combine_full_kernel,
        name="combine_full",
        out_shape=(
            jax.ShapeDtypeStruct((toks, width), BF),
            jax.ShapeDtypeStruct((toks, width), BF),
            jax.ShapeDtypeStruct((TOP, toks), F32),
        ),
        cost_estimate=pl.CostEstimate(
            flops=6 * toks * home.shape[0] * width, transcendentals=0, bytes_accessed=8 * 1024 * 1024
        ),
    )(home, places, values, grads, own, returned, dw_own, dw_back)


def shards(tokens, route, combine_weights, w_gate, w_up, w_down, grad_out):
    nodes = lax.axis_size("node")
    planes = lax.axis_size("local")
    toks, _ = tokens.shape
    up = [(i, (i + 1) % planes) for i in range(planes)]
    down = [(i, (i - 1) % planes) for i in range(planes)]
    across = [(i, (i + 2) % planes) for i in range(planes)]

    def send(value, pairs):
        return lax.ppermute(value, "local", pairs)

    def exchange(rows):
        return lax.all_to_all(rows, "node", split_axis=0, concat_axis=0, tiled=True)

    tokens_other, grads_other = send(tokens, across), send(grad_out, across)
    route_t = route.T
    weight_t = combine_weights.T
    small = send(jnp.concatenate([weight_t, route_t.astype(F32)], axis=0), across)
    weight_other = small[:TOP]
    route_other = small[TOP:].astype(jnp.int32)

    gate_t = jnp.swapaxes(w_gate, 1, 2)
    up_t = jnp.swapaxes(w_up, 1, 2)
    half = gate_t.shape[1] // 2

    def piece(expert, part):
        cut = slice(part * half, (part + 1) * half)
        return jnp.stack([gate_t[expert, cut], up_t[expert, cut], w_down[expert, cut]])

    p0a, p0b, p1a, p1b = piece(0, 0), piece(0, 1), piece(1, 0), piece(1, 1)
    w0 = [p0a, p0b, send(p0a, down), send(p0b, up)]
    below_a, above_b = send(p1a, up), send(p1b, down)
    below_b, above_a = send(p1b, up), send(p1a, down)
    far_a, far_b = send(below_a, up), send(above_b, down)
    w1 = [p1a, p1b, below_a, below_b, above_a, above_b, far_a, far_b]

    slot_own, slot_other = slots_of(route_t), slots_of(route_other)

    own_rows = dispatch(dispatch_own_kernel, nodes * OWN_ROWS, route_t, tokens, grad_out)
    arrived = exchange(own_rows)
    other_rows = dispatch(
        dispatch_other_kernel, nodes * OTHER_ROWS, route_t, route_other, tokens, grad_out, tokens_other, grads_other
    )
    arrived_other = exchange(other_rows)

    rows0 = expert_pair(arrived, arrived_other, w0, nodes)
    home0 = exchange(rows0)
    near = expert_near(arrived, arrived_other, w1[:6], nodes)
    rows1 = expert_far(near, w1[6:], nodes)
    home1 = exchange(rows1)

    own_even, other_even = route_t % 2 == 0, route_other % 2 == 0

    def places(route_rows, row, keep):
        chunk, index = row
        return jnp.where(keep, (route_rows // 2) * chunk + index, -1)

    def other_place(main, rest):
        index = jnp.where(slot_other < 8, main + slot_other, rest)
        return places(route_other, (OUT0_ROWS, index), other_even)

    def home_place(main, rest):
        index = jnp.where(slot_own < 8, main + slot_own, rest)
        return places(route_t, (OUT0_ROWS, index), own_even)

    def full_place(main, rest):
        index = jnp.where(slot_own < 8, main + slot_own, rest)
        return places(route_t, (OUT1_ROWS, index), ~own_even)

    def stacked(*parts):
        return jnp.concatenate([p.T for p in parts], axis=0)

    places0 = stacked(other_place(8, 33), other_place(24, 35), home_place(0, 32), home_place(16, 34))
    places1 = stacked(full_place(0, 16), full_place(8, 17))
    values0 = stacked(weight_other, weight_other, weight_t, weight_t)
    values1 = values0[2 * toks :]
    back, kept, dw_other, dw_own = combine_pair(home0, places0, values0, grad_out, grads_other)
    returned = send(back, across)
    dw_back = send(dw_other, across)
    combined, d_tokens, d_weights_t = combine_full(home1, places1, values1, grad_out, kept, returned, dw_own, dw_back)
    return combined, d_tokens, d_weights_t.T


def solution(mesh):
    tokens_spec = P(("node", "local"), None)

    return jax.shard_map(
        shards,
        mesh=mesh,
        in_specs=(
            tokens_spec,
            tokens_spec,
            tokens_spec,
            P("node", None, "local"),
            P("node", None, "local"),
            P("node", "local", None),
            tokens_spec,
        ),
        out_specs=(tokens_spec, tokens_spec, tokens_spec),
        check_vma=False,
    )
```

```python
import functools

import jax
import jax.numpy as jnp
from jax import lax
from jax.experimental import pallas as pl
from jax.experimental.pallas import tpu as pltpu
from jax.sharding import PartitionSpec as P

EXPERTS = 64
TOP = 4
BF = jnp.bfloat16
F32 = jnp.float32

OWN_ROWS = 32
OTHER_ROWS = 24
OUT0_ROWS = 40
OUT1_ROWS = 24


def slots_of(route_t):
    toks = route_t.shape[1]
    expert_ids = lax.broadcasted_iota(jnp.int32, (EXPERTS, toks), 0)
    hits = [(route_t[k : k + 1] == expert_ids) for k in range(TOP)]
    named = sum(jnp.where(h, 1.0, 0.0) for h in hits).astype(BF)
    from_ids = lax.broadcasted_iota(jnp.int32, (toks, toks), 0)
    to_ids = lax.broadcasted_iota(jnp.int32, (toks, toks), 1)
    before = jnp.where(from_ids < to_ids, 1.0, 0.0).astype(BF)
    earlier = jnp.dot(named, before, preferred_element_type=F32)
    slots = [jnp.sum(jnp.where(h, earlier, 0.0), axis=0, keepdims=True) for h in hits]
    return jnp.concatenate(slots, axis=0).astype(jnp.int32)


def dispatch_rows(pairs, block, first):
    total = None
    for places, values in pairs:
        ids = lax.broadcasted_iota(jnp.int32, (block, places.shape[1]), 0) + first
        hot = jnp.zeros(ids.shape, F32)
        for k in range(TOP):
            hot = hot + jnp.where(places[k : k + 1] == ids, 1.0, 0.0)
        term = jnp.dot(hot.astype(BF), values, preferred_element_type=F32)
        total = term if total is None else total + term
    return total.astype(BF)


def dispatch_own_kernel(route_ref, tokens, grads, rows):
    block = rows.shape[0]
    first = pl.program_id(0) * block
    route = route_ref[...]
    slot = slots_of(route)
    base = (route // 2) * OWN_ROWS + (route % 2) * 16 + slot
    kept = slot < 8
    x_place, g_place = jnp.where(kept, base, -1), jnp.where(kept, base + 8, -1)
    rows[...] = dispatch_rows([(x_place, tokens[...]), (g_place, grads[...])], block, first)


def dispatch_other_kernel(route_ref, route_other_ref, tokens, grads, tokens_other, grads_other, rows):
    block = rows.shape[0]
    first = pl.program_id(0) * block
    route = route_ref[...]
    odd = route % 2
    ninth = slots_of(route) == 8
    base = (route // 2) * OTHER_ROWS
    x_place = jnp.where(ninth, base + 16 + 4 * odd, -1)
    g_place = jnp.where(ninth, base + 18 + 3 * odd, -1)
    route = route_other_ref[...]
    even = route % 2 == 0
    slot = slots_of(route)
    base = (route // 2) * OTHER_ROWS
    x_far = jnp.where(even, base + jnp.where(slot < 8, slot, 17), -1)
    g_far = jnp.where(even, base + jnp.where(slot < 8, slot + 8, 19), -1)
    rows[...] = dispatch_rows(
        [(x_place, tokens[...]), (g_place, grads[...]), (x_far, tokens_other[...]), (g_far, grads_other[...])],
        block,
        first,
    )


def dispatch(kernel, rows, *args):
    width = args[-1].shape[1]
    steps = 4

    def whole(x):
        return pl.BlockSpec(x.shape, lambda i: (0, 0))

    return pl.pallas_call(
        kernel,
        grid=(steps,),
        out_shape=jax.ShapeDtypeStruct((rows, width), BF),
        in_specs=[whole(x) for x in args],
        out_specs=pl.BlockSpec((rows // steps, width), lambda i: (i, 0)),
        cost_estimate=pl.CostEstimate(
            flops=4 * rows * 128 * width, transcendentals=0, bytes_accessed=4 * rows * width
        ),
    )(*args)


def landed(dst, sem):
    pltpu.make_async_copy(dst, dst, sem).wait()


def fetch_rows(nodes, src, stride, first, dst, at, sem):
    def step(n, carry):
        frm = src.at[pl.ds(pl.multiple_of(n * stride + first, 8), 8)]
        to = dst.at[pl.ds(pl.multiple_of(at + n * 8, 8), 8)]
        pltpu.make_async_copy(frm, to, sem).start()
        return carry

    lax.fori_loop(0, nodes, step, 0)


def put_rows(nodes, src, at, dst, stride, first, sem):
    def step(n, carry):
        frm = src.at[pl.ds(pl.multiple_of(at + n * 8, 8), 8)]
        to = dst.at[pl.ds(pl.multiple_of(n * stride + first, 8), 8)]
        pltpu.make_async_copy(frm, to, sem).start()
        return carry

    lax.fori_loop(0, nodes, step, 0)


def fetch_weights(pieces, weights, sems, first):
    part = pieces[0].shape[1]
    for j, w in enumerate(weights):
        for i, p in enumerate(pieces):
            pltpu.make_async_copy(p.at[j], w.at[pl.ds(i * part, part)], sems.at[first + j]).start()


def picked(nodes, extra, offset, out_major):
    shape = (nodes * 8, nodes * extra) if out_major else (nodes * extra, nodes * 8)
    compact = lax.broadcasted_iota(jnp.int32, shape, 1 if out_major else 0)
    wide = lax.broadcasted_iota(jnp.int32, shape, 0 if out_major else 1)
    want = (compact // extra) * 8 + offset + compact % extra
    return (want == wide).astype(F32).astype(BF)


def by_hidden(rows, w):
    return lax.dot_general(rows, w, (((1,), (1,)), ((), ())), preferred_element_type=F32)


def by_row(rows, w):
    return jnp.dot(rows, w, preferred_element_type=F32)


def inner(x, g, wg, wu, wd):
    gate = by_hidden(x, wg)
    upper = by_hidden(x, wu)
    d_hidden = by_hidden(g, wd)
    s = jax.nn.sigmoid(gate)
    act = gate * s
    hidden = (act * upper).astype(BF)
    d_gate = (d_hidden * upper * s * (1.0 + gate * (1.0 - s))).astype(BF)
    d_up = (d_hidden * act).astype(BF)
    return hidden, d_gate, d_up


def expert_pair_kernel(nodes, n_pieces, *refs):
    arrived, arrived_other, pieces, home = refs[0], refs[1], refs[2 : 2 + n_pieces], refs[2 + n_pieces]
    xs, gs, rest, wg, wu, wd, outs, backs, out_rest, sems = refs[3 + n_pieces :]
    main, small = nodes * 16, nodes * 2
    fetch_rows(nodes, arrived, OWN_ROWS, 0, xs, 0, sems.at[0])
    fetch_rows(nodes, arrived_other, OTHER_ROWS, 0, xs, nodes * 8, sems.at[0])
    fetch_rows(nodes, arrived_other, OTHER_ROWS, 16, rest, 0, sems.at[1])
    fetch_weights(pieces, (wg, wu, wd), sems, 3)
    fetch_rows(nodes, arrived, OWN_ROWS, 8, gs, 0, sems.at[2])
    fetch_rows(nodes, arrived_other, OTHER_ROWS, 8, gs, nodes * 8, sems.at[2])
    landed(rest, sems.at[1])
    xs[pl.ds(main, small)] = by_row(picked(nodes, 2, 0, False), rest[...]).astype(BF)
    gs[pl.ds(main, small)] = by_row(picked(nodes, 2, 2, False), rest[...]).astype(BF)
    landed(xs.at[pl.ds(0, main)], sems.at[0])
    landed(wg, sems.at[3])
    landed(wu, sems.at[4])
    landed(gs.at[pl.ds(0, main)], sems.at[2])
    landed(wd, sems.at[5])
    size = (main + small) // 2

    def block(b, carry):
        at = pl.ds(pl.multiple_of(b * size, 16), size)
        hidden, d_gate, d_up = inner(xs[at], gs[at], wg[...], wu[...], wd[...])
        outs[at] = by_row(hidden, wd[...]).astype(BF)
        backs[at] = (by_row(d_gate, wg[...]) + by_row(d_up, wu[...])).astype(BF)
        return carry

    lax.fori_loop(0, 2, block, 0)
    put_rows(nodes, outs, 0, home, OUT0_ROWS, 0, sems.at[0])
    put_rows(nodes, outs, nodes * 8, home, OUT0_ROWS, 8, sems.at[0])
    put_rows(nodes, backs, 0, home, OUT0_ROWS, 16, sems.at[1])
    put_rows(nodes, backs, nodes * 8, home, OUT0_ROWS, 24, sems.at[1])
    out_rest[...] = (
        by_row(picked(nodes, 2, 0, True), outs[pl.ds(main, small)])
        + by_row(picked(nodes, 2, 2, True), backs[pl.ds(main, small)])
    ).astype(BF)
    put_rows(nodes, out_rest, 0, home, OUT0_ROWS, 32, sems.at[2])
    landed(outs.at[pl.ds(0, main)], sems.at[0])
    landed(backs.at[pl.ds(0, main)], sems.at[1])
    landed(out_rest, sems.at[2])


def expert_near_kernel(nodes, n_pieces, *refs):
    arrived, arrived_other, pieces = refs[0], refs[1], refs[2 : 2 + n_pieces]
    out_part, back_part, xs, gs = refs[2 + n_pieces : 6 + n_pieces]
    rest, wg, wu, wd, sems = refs[6 + n_pieces :]
    main, small = nodes * 8, nodes
    fetch_rows(nodes, arrived, OWN_ROWS, 16, xs, 0, sems.at[0])
    fetch_rows(nodes, arrived, OWN_ROWS, 24, gs, 0, sems.at[2])
    fetch_rows(nodes, arrived_other, OTHER_ROWS, 16, rest, 0, sems.at[1])
    fetch_weights(pieces, (wg, wu, wd), sems, 3)
    landed(rest, sems.at[1])
    landed(xs.at[pl.ds(0, main)], sems.at[0])
    landed(gs.at[pl.ds(0, main)], sems.at[2])
    xs[pl.ds(main, small)] = by_row(picked(nodes, 1, 4, False), rest[...]).astype(BF)
    gs[pl.ds(main, small)] = by_row(picked(nodes, 1, 5, False), rest[...]).astype(BF)
    landed(wg, sems.at[3])
    landed(wu, sems.at[4])
    landed(wd, sems.at[5])
    size = (main + small) // 2

    def block(b, carry):
        at = pl.ds(pl.multiple_of(b * size, 16), size)
        hidden, d_gate, d_up = inner(xs[at], gs[at], wg[...], wu[...], wd[...])
        out_part[at] = by_row(hidden, wd[...])
        back_part[at] = by_row(d_gate, wg[...]) + by_row(d_up, wu[...])
        return carry

    lax.fori_loop(0, 2, block, 0)


def expert_far_kernel(nodes, n_pieces, *refs):
    xs, gs, out_at, back_at = refs[:4]
    pieces, home = refs[4 : 4 + n_pieces], refs[4 + n_pieces]
    out_part, back_part, wg, wu, wd, outs, backs, out_rest, sems = refs[5 + n_pieces :]
    main, small = nodes * 8, nodes
    fetch_weights(pieces, (wg, wu, wd), sems, 3)
    pltpu.make_async_copy(out_at, out_part, sems.at[6]).start()
    pltpu.make_async_copy(back_at, back_part, sems.at[7]).start()
    landed(wg, sems.at[3])
    landed(wu, sems.at[4])
    landed(wd, sems.at[5])
    hidden, d_gate, d_up = inner(xs[...], gs[...], wg[...], wu[...], wd[...])
    landed(out_part, sems.at[6])
    outs[...] = (by_row(hidden, wd[...]) + out_part[...]).astype(BF)
    put_rows(nodes, outs, 0, home, OUT1_ROWS, 0, sems.at[0])
    landed(back_part, sems.at[7])
    backs[...] = (by_row(d_gate, wg[...]) + by_row(d_up, wu[...]) + back_part[...]).astype(BF)
    put_rows(nodes, backs, 0, home, OUT1_ROWS, 8, sems.at[1])
    out_rest[...] = (
        by_row(picked(nodes, 1, 0, True), outs[pl.ds(main, small)])
        + by_row(picked(nodes, 1, 1, True), backs[pl.ds(main, small)])
    ).astype(BF)
    put_rows(nodes, out_rest, 0, home, OUT1_ROWS, 16, sems.at[2])
    landed(outs.at[pl.ds(0, main)], sems.at[0])
    landed(backs.at[pl.ds(0, main)], sems.at[1])
    landed(out_rest, sems.at[2])


def on_chip(value):
    return pltpu.with_memory_space_constraint(value, pltpu.VMEM)


ANY = pl.BlockSpec(memory_space=pltpu.HBM)
WHOLE = pl.BlockSpec(memory_space=pltpu.VMEM)


def room(mib):
    return pltpu.CompilerParams(vmem_limit_bytes=mib * 1024 * 1024)


def expert_cost(rows, hidden, width):
    return pl.CostEstimate(
        flops=12 * rows * hidden * width,
        transcendentals=rows * hidden,
        bytes_accessed=2 * width * (4 * rows + 3 * hidden),
    )


def expert_pair(arrived, arrived_other, pieces, nodes):
    width = arrived.shape[1]
    rows, hidden = nodes * 18, len(pieces) * pieces[0].shape[1]
    scratch = [(rows, width), (rows, width), (nodes * 8, width)] + [(hidden, width)] * 3
    scratch += [(rows, width), (rows, width), (nodes * 8, width)]
    return pl.pallas_call(
        functools.partial(expert_pair_kernel, nodes, len(pieces)),
        name="expert_pair",
        out_shape=jax.ShapeDtypeStruct((nodes * OUT0_ROWS, width), BF),
        in_specs=[ANY, WHOLE] + [ANY] * len(pieces),
        out_specs=ANY,
        scratch_shapes=[pltpu.VMEM(s, BF) for s in scratch] + [pltpu.SemaphoreType.DMA((6,))],
        compiler_params=room(46),
        cost_estimate=expert_cost(rows, hidden, width),
    )(arrived, arrived_other, *pieces)


def expert_near(arrived, arrived_other, pieces, nodes):
    width = arrived.shape[1]
    rows, hidden = nodes * 9, len(pieces) * pieces[0].shape[1]
    scratch = [(nodes * 8, width)] + [(hidden, width)] * 3
    return pl.pallas_call(
        functools.partial(expert_near_kernel, nodes, len(pieces)),
        name="expert_near",
        out_shape=tuple(jax.ShapeDtypeStruct((rows, width), t) for t in (F32, F32, BF, BF)),
        in_specs=[ANY, WHOLE] + [ANY] * len(pieces),
        out_specs=(WHOLE,) * 4,
        scratch_shapes=[pltpu.VMEM(s, BF) for s in scratch] + [pltpu.SemaphoreType.DMA((6,))],
        compiler_params=room(46),
        cost_estimate=expert_cost(rows, hidden, width),
    )(arrived, arrived_other, *pieces)


def expert_far(near, pieces, nodes):
    out_part, back_part, xs, gs = near
    rows, width = xs.shape
    hidden = len(pieces) * pieces[0].shape[1]
    scratch = [((rows, width), F32)] * 2 + [((hidden, width), BF)] * 3
    scratch += [((rows, width), BF)] * 2 + [((nodes * 8, width), BF)]
    return pl.pallas_call(
        functools.partial(expert_far_kernel, nodes, len(pieces)),
        name="expert_far",
        out_shape=jax.ShapeDtypeStruct((nodes * OUT1_ROWS, width), BF),
        in_specs=[WHOLE] * 2 + [ANY] * (2 + len(pieces)),
        out_specs=ANY,
        scratch_shapes=[pltpu.VMEM(s, t) for s, t in scratch] + [pltpu.SemaphoreType.DMA((8,))],
        compiler_params=room(57),
        cost_estimate=expert_cost(rows, hidden, width),
    )(on_chip(xs), on_chip(gs), out_part, back_part, *pieces)


def mixed(rows, places, values):
    ids = lax.broadcasted_iota(jnp.int32, (places.shape[0], rows.shape[0]), 1)
    total = jnp.zeros(ids.shape, F32)
    for k in range(TOP):
        total = total + jnp.where(places[:, k : k + 1] == ids, values[:, k : k + 1], 0.0)
    return jnp.dot(total.astype(BF), rows, preferred_element_type=F32)


def weight_grads(rows, grads, places):
    table = lax.dot_general(grads, rows, (((1,), (1,)), ((), ())), preferred_element_type=F32)
    ids = lax.broadcasted_iota(jnp.int32, table.shape, 1)
    lane = lax.broadcasted_iota(jnp.int32, (table.shape[0], 128), 1)
    result = jnp.zeros(lane.shape, F32)
    for k in range(TOP):
        column = jnp.sum(jnp.where(places[:, k : k + 1] == ids, table, 0.0), axis=1, keepdims=True)
        result = result + jnp.where(lane == k, column, 0.0)
    return result


def combine_pair_kernel(home, places_ref, values_ref, grads, grads_other, back, own, dw_other, dw_own):
    toks = grads.shape[0]
    rows = home[...]
    total = mixed(rows, places_ref[...], values_ref[...])
    back[...] = total[: 2 * toks].astype(BF)
    own[...] = total[2 * toks :]
    dw_other[...] = jnp.transpose(weight_grads(rows, grads_other[...], places_ref[:toks]))[:8]
    dw_own[...] = jnp.transpose(weight_grads(rows, grads[...], places_ref[2 * toks : 3 * toks]))[:8]


def combine_full_kernel(
    home, places_ref, values_ref, dw_own, dw_back, grads_at, own_at, returned_at, combined, d_tokens, d_weights, *scratch
):
    grads, own, returned, sems = scratch
    toks = grads.shape[0]
    copies = [
        pltpu.make_async_copy(src, dst, sems.at[i])
        for i, (src, dst) in enumerate(((own_at, own), (returned_at, returned), (grads_at, grads)))
    ]
    for copy in copies:
        copy.start()
    rows = home[...]
    total = mixed(rows, places_ref[...], values_ref[...])
    copies[0].wait()
    copies[1].wait()
    total = total + own[...] + returned[...].astype(F32)
    combined[...] = total[:toks].astype(BF)
    d_tokens[...] = total[toks:].astype(BF)
    copies[2].wait()
    dw = jnp.transpose(weight_grads(rows, grads[...], places_ref[:toks]))[:8] + dw_own[...] + dw_back[...]
    d_weights[...] = dw[:TOP]


def combine_pair(home, places, values, grads, grads_other):
    toks, width = grads.shape
    return pl.pallas_call(
        combine_pair_kernel,
        name="combine_pair",
        out_shape=(
            jax.ShapeDtypeStruct((2 * toks, width), BF),
            jax.ShapeDtypeStruct((2 * toks, width), F32),
            jax.ShapeDtypeStruct((8, toks), F32),
            jax.ShapeDtypeStruct((8, toks), F32),
        ),
        compiler_params=room(60),
        cost_estimate=pl.CostEstimate(
            flops=12 * toks * home.shape[0] * width, transcendentals=0, bytes_accessed=12 * 1024 * 1024
        ),
    )(home, places, values, grads, grads_other)


def combine_full(home, places, values, grads, own, returned, dw_own, dw_back):
    toks, width = grads.shape
    return pl.pallas_call(
        combine_full_kernel,
        name="combine_full",
        out_shape=(
            jax.ShapeDtypeStruct((toks, width), BF),
            jax.ShapeDtypeStruct((toks, width), BF),
            jax.ShapeDtypeStruct((TOP, toks), F32),
        ),
        in_specs=[WHOLE] * 5 + [ANY] * 3,
        out_specs=(WHOLE,) * 3,
        scratch_shapes=[
            pltpu.VMEM((toks, width), BF),
            pltpu.VMEM((2 * toks, width), F32),
            pltpu.VMEM((2 * toks, width), BF),
            pltpu.SemaphoreType.DMA((3,)),
        ],
        compiler_params=room(60),
        cost_estimate=pl.CostEstimate(
            flops=6 * toks * home.shape[0] * width, transcendentals=0, bytes_accessed=8 * 1024 * 1024
        ),
    )(on_chip(home), places, values, dw_own, dw_back, grads, own, returned)


def shards(tokens, route, combine_weights, w_gate, w_up, w_down, grad_out):
    nodes = lax.axis_size("node")
    planes = lax.axis_size("local")
    toks, _ = tokens.shape
    up = [(i, (i + 1) % planes) for i in range(planes)]
    down = [(i, (i - 1) % planes) for i in range(planes)]
    across = [(i, (i + 2) % planes) for i in range(planes)]

    def send(value, pairs):
        return lax.ppermute(value, "local", pairs)

    def exchange(rows):
        return lax.all_to_all(rows, "node", split_axis=0, concat_axis=0, tiled=True)

    tokens_other, grads_other = send(tokens, across), send(grad_out, across)
    route_t = route.T
    weight_t = combine_weights.T
    small = send(jnp.concatenate([weight_t, route_t.astype(F32)], axis=0), across)
    weight_other = small[:TOP]
    route_other = small[TOP:].astype(jnp.int32)

    gate_t = jnp.swapaxes(w_gate, 1, 2)
    up_t = jnp.swapaxes(w_up, 1, 2)
    half = gate_t.shape[1] // 2

    def piece(expert, part):
        cut = slice(part * half, (part + 1) * half)
        return jnp.stack([gate_t[expert, cut], up_t[expert, cut], w_down[expert, cut]])

    p0a, p0b, p1a, p1b = piece(0, 0), piece(0, 1), piece(1, 0), piece(1, 1)
    w0 = [p0a, p0b, send(p0a, down), send(p0b, up)]
    below_a, above_b = send(p1a, up), send(p1b, down)
    below_b, above_a = send(p1b, up), send(p1a, down)
    far_a, far_b = send(below_a, up), send(above_b, down)
    w1 = [p1a, p1b, below_a, below_b, above_a, above_b, far_a, far_b]

    slot_own, slot_other = slots_of(route_t), slots_of(route_other)

    own_rows = dispatch(dispatch_own_kernel, nodes * OWN_ROWS, route_t, tokens, grad_out)
    arrived = exchange(own_rows)
    other_rows = dispatch(
        dispatch_other_kernel, nodes * OTHER_ROWS, route_t, route_other, tokens, grad_out, tokens_other, grads_other
    )
    arrived_other = exchange(other_rows)

    arrived_other = on_chip(arrived_other)
    rows0 = expert_pair(arrived, arrived_other, w0, nodes)
    home0 = exchange(rows0)
    near = expert_near(arrived, arrived_other, w1[:6], nodes)
    rows1 = expert_far(near, w1[6:], nodes)
    home1 = exchange(rows1)

    own_even, other_even = route_t % 2 == 0, route_other % 2 == 0

    def places(route_rows, row, keep):
        chunk, index = row
        return jnp.where(keep, (route_rows // 2) * chunk + index, -1)

    def other_place(main, rest):
        index = jnp.where(slot_other < 8, main + slot_other, rest)
        return places(route_other, (OUT0_ROWS, index), other_even)

    def home_place(main, rest):
        index = jnp.where(slot_own < 8, main + slot_own, rest)
        return places(route_t, (OUT0_ROWS, index), own_even)

    def full_place(main, rest):
        index = jnp.where(slot_own < 8, main + slot_own, rest)
        return places(route_t, (OUT1_ROWS, index), ~own_even)

    def stacked(*parts):
        return jnp.concatenate([p.T for p in parts], axis=0)

    places0 = stacked(other_place(8, 33), other_place(24, 35), home_place(0, 32), home_place(16, 34))
    places1 = stacked(full_place(0, 16), full_place(8, 17))
    values0 = stacked(weight_other, weight_other, weight_t, weight_t)
    values1 = values0[2 * toks :]
    back, kept, dw_other, dw_own = combine_pair(home0, places0, values0, grad_out, grads_other)
    returned = send(back, across)
    dw_back = send(dw_other, across)
    combined, d_tokens, d_weights_t = combine_full(home1, places1, values1, grad_out, kept, returned, dw_own, dw_back)
    return combined, d_tokens, d_weights_t.T


def solution(mesh):
    tokens_spec = P(("node", "local"), None)

    return jax.shard_map(
        shards,
        mesh=mesh,
        in_specs=(
            tokens_spec,
            tokens_spec,
            tokens_spec,
            P("node", None, "local"),
            P("node", None, "local"),
            P("node", "local", None),
            tokens_spec,
        ),
        out_specs=(tokens_spec, tokens_spec, tokens_spec),
        check_vma=False,
    )
```

```python
import functools

import jax
import jax.numpy as jnp
from jax import lax
from jax.experimental import pallas as pl
from jax.experimental.pallas import tpu as pltpu
from jax.sharding import PartitionSpec as P

EXPERTS = 64
TOP = 4
BF = jnp.bfloat16
F32 = jnp.float32

OWN_ROWS = 32
OTHER_ROWS = 24
OUT0_ROWS = 40
OUT1_ROWS = 16


def slots_of(route_t):
    toks = route_t.shape[1]
    expert_ids = lax.broadcasted_iota(jnp.int32, (EXPERTS, toks), 0)
    hits = [(route_t[k : k + 1] == expert_ids) for k in range(TOP)]
    named = sum(jnp.where(h, 1.0, 0.0) for h in hits).astype(BF)
    from_ids = lax.broadcasted_iota(jnp.int32, (toks, toks), 0)
    to_ids = lax.broadcasted_iota(jnp.int32, (toks, toks), 1)
    before = jnp.where(from_ids < to_ids, 1.0, 0.0).astype(BF)
    earlier = jnp.dot(named, before, preferred_element_type=F32)
    slots = [jnp.sum(jnp.where(h, earlier, 0.0), axis=0, keepdims=True) for h in hits]
    return jnp.concatenate(slots, axis=0).astype(jnp.int32)


def dispatch_rows(pairs, block, first):
    total = None
    for places, values in pairs:
        ids = lax.broadcasted_iota(jnp.int32, (block, places.shape[1]), 0) + first
        hot = jnp.zeros(ids.shape, F32)
        for k in range(TOP):
            hot = hot + jnp.where(places[k : k + 1] == ids, 1.0, 0.0)
        term = jnp.dot(hot.astype(BF), values, preferred_element_type=F32)
        total = term if total is None else total + term
    return total.astype(BF)


def dispatch_own_kernel(route_ref, tokens, grads, rows):
    block = rows.shape[0]
    first = pl.program_id(0) * block
    route = route_ref[...]
    slot = slots_of(route)
    base = (route // 2) * OWN_ROWS + (route % 2) * 16 + slot
    kept = slot < 8
    x_place, g_place = jnp.where(kept, base, -1), jnp.where(kept, base + 8, -1)
    rows[...] = dispatch_rows([(x_place, tokens[...]), (g_place, grads[...])], block, first)


def dispatch_other_kernel(route_ref, route_other_ref, tokens, grads, tokens_other, grads_other, rows):
    block = rows.shape[0]
    first = pl.program_id(0) * block
    route = route_ref[...]
    odd = route % 2
    ninth = slots_of(route) == 8
    base = (route // 2) * OTHER_ROWS
    x_place = jnp.where(ninth, base + 16 + 4 * odd, -1)
    g_place = jnp.where(ninth, base + 18 + 4 * odd, -1)
    route = route_other_ref[...]
    odd = route % 2
    slot = slots_of(route)
    ninth = slot == 8
    base = (route // 2) * OTHER_ROWS
    kept = (odd == 0) | ninth
    x_far = jnp.where(kept, base + jnp.where(ninth, 17 + 4 * odd, slot), -1)
    g_far = jnp.where(kept, base + jnp.where(ninth, 19 + 4 * odd, slot + 8), -1)
    rows[...] = dispatch_rows(
        [(x_place, tokens[...]), (g_place, grads[...]), (x_far, tokens_other[...]), (g_far, grads_other[...])],
        block,
        first,
    )


def dispatch(kernel, rows, *args):
    width = args[-1].shape[1]
    steps = 4

    def whole(x):
        return pl.BlockSpec(x.shape, lambda i: (0, 0))

    return pl.pallas_call(
        kernel,
        grid=(steps,),
        out_shape=jax.ShapeDtypeStruct((rows, width), BF),
        in_specs=[whole(x) for x in args],
        out_specs=pl.BlockSpec((rows // steps, width), lambda i: (i, 0)),
        cost_estimate=pl.CostEstimate(
            flops=4 * rows * 128 * width, transcendentals=0, bytes_accessed=4 * rows * width
        ),
    )(*args)


def landed(dst, sem):
    pltpu.make_async_copy(dst, dst, sem).wait()


def fetch_rows(nodes, src, stride, first, dst, at, sem):
    def step(n, carry):
        frm = src.at[pl.ds(pl.multiple_of(n * stride + first, 8), 8)]
        to = dst.at[pl.ds(pl.multiple_of(at + n * 8, 8), 8)]
        pltpu.make_async_copy(frm, to, sem).start()
        return carry

    lax.fori_loop(0, nodes, step, 0)


def put_rows(nodes, src, at, dst, stride, first, sem):
    def step(n, carry):
        frm = src.at[pl.ds(pl.multiple_of(at + n * 8, 8), 8)]
        to = dst.at[pl.ds(pl.multiple_of(n * stride + first, 8), 8)]
        pltpu.make_async_copy(frm, to, sem).start()
        return carry

    lax.fori_loop(0, nodes, step, 0)


def fetch_weights(pieces, weights, sems, first):
    part = pieces[0].shape[1]
    for j, w in enumerate(weights):
        for i, p in enumerate(pieces):
            pltpu.make_async_copy(p.at[j], w.at[pl.ds(i * part, part)], sems.at[first + j]).start()


def picked(nodes, extra, offset, out_major):
    shape = (nodes * 8, nodes * extra) if out_major else (nodes * extra, nodes * 8)
    compact = lax.broadcasted_iota(jnp.int32, shape, 1 if out_major else 0)
    wide = lax.broadcasted_iota(jnp.int32, shape, 0 if out_major else 1)
    want = (compact // extra) * 8 + offset + compact % extra
    return (want == wide).astype(F32).astype(BF)


def by_hidden(rows, w):
    return lax.dot_general(rows, w, (((1,), (1,)), ((), ())), preferred_element_type=F32)


def by_row(rows, w):
    return jnp.dot(rows, w, preferred_element_type=F32)


def inner(x, g, wg, wu, wd):
    gate = by_hidden(x, wg)
    upper = by_hidden(x, wu)
    d_hidden = by_hidden(g, wd)
    s = jax.nn.sigmoid(gate)
    act = gate * s
    hidden = (act * upper).astype(BF)
    d_gate = (d_hidden * upper * s * (1.0 + gate * (1.0 - s))).astype(BF)
    d_up = (d_hidden * act).astype(BF)
    return hidden, d_gate, d_up


def expert_pair_kernel(nodes, n_pieces, *refs):
    arrived, arrived_other, pieces = refs[0], refs[1], refs[2 : 2 + n_pieces]
    home, ninth_out, ninth_back = refs[2 + n_pieces : 5 + n_pieces]
    xs, gs, rest, wg, wu, wd, outs, backs, sems = refs[5 + n_pieces :]
    main, small = nodes * 16, nodes * 2
    fetch_rows(nodes, arrived, OWN_ROWS, 0, xs, 0, sems.at[0])
    fetch_rows(nodes, arrived_other, OTHER_ROWS, 0, xs, nodes * 8, sems.at[0])
    fetch_rows(nodes, arrived_other, OTHER_ROWS, 16, rest, 0, sems.at[1])
    fetch_weights(pieces, (wg, wu, wd), sems, 3)
    fetch_rows(nodes, arrived, OWN_ROWS, 8, gs, 0, sems.at[2])
    fetch_rows(nodes, arrived_other, OTHER_ROWS, 8, gs, nodes * 8, sems.at[2])
    landed(rest, sems.at[1])
    xs[pl.ds(main, small)] = by_row(picked(nodes, 2, 0, False), rest[...]).astype(BF)
    gs[pl.ds(main, small)] = by_row(picked(nodes, 2, 2, False), rest[...]).astype(BF)
    landed(xs.at[pl.ds(0, main)], sems.at[0])
    landed(wg, sems.at[3])
    landed(wu, sems.at[4])
    landed(gs.at[pl.ds(0, main)], sems.at[2])
    landed(wd, sems.at[5])
    size = (main + small) // 3

    def block(b, carry):
        at = pl.ds(pl.multiple_of(b * size, 16), size)
        hidden, d_gate, d_up = inner(xs[at], gs[at], wg[...], wu[...], wd[...])
        outs[at] = by_row(hidden, wd[...]).astype(BF)
        backs[at] = (by_row(d_gate, wg[...]) + by_row(d_up, wu[...])).astype(BF)
        return carry

    lax.fori_loop(0, 3, block, 0)
    put_rows(nodes, outs, 0, home, OUT0_ROWS, 0, sems.at[0])
    put_rows(nodes, outs, nodes * 8, home, OUT0_ROWS, 8, sems.at[0])
    put_rows(nodes, backs, 0, home, OUT0_ROWS, 16, sems.at[1])
    put_rows(nodes, backs, nodes * 8, home, OUT0_ROWS, 24, sems.at[1])
    ninth_out[...] = outs[pl.ds(main, small)]
    ninth_back[...] = backs[pl.ds(main, small)]
    landed(outs.at[pl.ds(0, main)], sems.at[0])
    landed(backs.at[pl.ds(0, main)], sems.at[1])


def expert_ninth_kernel(nodes, n_pieces, *refs):
    arrived_other, pair_out, pair_back, pieces = refs[0], refs[1], refs[2], refs[3 : 3 + n_pieces]
    home = refs[4 + n_pieces]
    rest, wg, wu, wd, out_rest, sems = refs[5 + n_pieces :]
    fetch_rows(nodes, arrived_other, OTHER_ROWS, 16, rest, 0, sems.at[1])
    fetch_weights(pieces, (wg, wu, wd), sems, 3)
    landed(rest, sems.at[1])
    xs = by_row(picked(nodes, 2, 4, False), rest[...]).astype(BF)
    gs = by_row(picked(nodes, 2, 6, False), rest[...]).astype(BF)
    carried = by_row(picked(nodes, 2, 0, True), pair_out[...]) + by_row(picked(nodes, 2, 2, True), pair_back[...])
    landed(wg, sems.at[3])
    landed(wu, sems.at[4])
    landed(wd, sems.at[5])
    hidden, d_gate, d_up = inner(xs, gs, wg[...], wu[...], wd[...])
    out = by_row(hidden, wd[...]).astype(BF)
    back = (by_row(d_gate, wg[...]) + by_row(d_up, wu[...])).astype(BF)
    out_rest[...] = (
        carried + by_row(picked(nodes, 2, 4, True), out) + by_row(picked(nodes, 2, 6, True), back)
    ).astype(BF)
    put_rows(nodes, out_rest, 0, home, OUT0_ROWS, 32, sems.at[2])
    landed(out_rest, sems.at[2])


def expert_near_kernel(nodes, n_pieces, *refs):
    arrived, pieces = refs[0], refs[1 : 1 + n_pieces]
    out_part, back_part, xs, gs = refs[1 + n_pieces : 5 + n_pieces]
    wg, wu, wd, sems = refs[5 + n_pieces :]
    fetch_rows(nodes, arrived, OWN_ROWS, 16, xs, 0, sems.at[0])
    fetch_rows(nodes, arrived, OWN_ROWS, 24, gs, 0, sems.at[2])
    fetch_weights(pieces, (wg, wu, wd), sems, 3)
    landed(xs, sems.at[0])
    landed(gs, sems.at[2])
    landed(wg, sems.at[3])
    landed(wu, sems.at[4])
    landed(wd, sems.at[5])
    size = nodes * 4

    def block(b, carry):
        at = pl.ds(pl.multiple_of(b * size, 16), size)
        hidden, d_gate, d_up = inner(xs[at], gs[at], wg[...], wu[...], wd[...])
        out_part[at] = by_row(hidden, wd[...])
        back_part[at] = by_row(d_gate, wg[...]) + by_row(d_up, wu[...])
        return carry

    lax.fori_loop(0, 2, block, 0)


def expert_far_kernel(nodes, n_pieces, *refs):
    xs, gs, out_at, back_at = refs[:4]
    pieces, home = refs[4 : 4 + n_pieces], refs[4 + n_pieces]
    out_part, back_part, wg, wu, wd, outs, backs, sems = refs[5 + n_pieces :]
    fetch_weights(pieces, (wg, wu, wd), sems, 3)
    pltpu.make_async_copy(out_at, out_part, sems.at[6]).start()
    pltpu.make_async_copy(back_at, back_part, sems.at[7]).start()
    landed(wg, sems.at[3])
    landed(wu, sems.at[4])
    landed(wd, sems.at[5])
    hidden, d_gate, d_up = inner(xs[...], gs[...], wg[...], wu[...], wd[...])
    landed(out_part, sems.at[6])
    outs[...] = (by_row(hidden, wd[...]) + out_part[...]).astype(BF)
    put_rows(nodes, outs, 0, home, OUT1_ROWS, 0, sems.at[0])
    landed(back_part, sems.at[7])
    backs[...] = (by_row(d_gate, wg[...]) + by_row(d_up, wu[...]) + back_part[...]).astype(BF)
    put_rows(nodes, backs, 0, home, OUT1_ROWS, 8, sems.at[1])
    landed(outs, sems.at[0])
    landed(backs, sems.at[1])


def on_chip(value):
    return pltpu.with_memory_space_constraint(value, pltpu.VMEM)


ANY = pl.BlockSpec(memory_space=pltpu.HBM)
WHOLE = pl.BlockSpec(memory_space=pltpu.VMEM)


def room(mib):
    return pltpu.CompilerParams(vmem_limit_bytes=mib * 1024 * 1024)


def expert_cost(rows, hidden, width):
    return pl.CostEstimate(
        flops=12 * rows * hidden * width,
        transcendentals=rows * hidden,
        bytes_accessed=2 * width * (4 * rows + 3 * hidden),
    )


def expert_pair(arrived, arrived_other, pieces, nodes):
    width = arrived.shape[1]
    rows, hidden = nodes * 18, len(pieces) * pieces[0].shape[1]
    ninth = jax.ShapeDtypeStruct((nodes * 2, width), BF)
    scratch = [(rows, width), (rows, width), (nodes * 8, width)] + [(hidden, width)] * 3
    scratch += [(rows, width), (rows, width)]
    return pl.pallas_call(
        functools.partial(expert_pair_kernel, nodes, len(pieces)),
        name="expert_pair",
        out_shape=(jax.ShapeDtypeStruct((nodes * OUT0_ROWS, width), BF), ninth, ninth),
        in_specs=[ANY, WHOLE] + [ANY] * len(pieces),
        out_specs=(ANY, WHOLE, WHOLE),
        scratch_shapes=[pltpu.VMEM(s, BF) for s in scratch] + [pltpu.SemaphoreType.DMA((6,))],
        compiler_params=room(46),
        cost_estimate=expert_cost(rows, hidden, width),
    )(arrived, arrived_other, *pieces)


def expert_ninth(arrived_other, pair_rows, pieces, nodes):
    home, pair_out, pair_back = pair_rows
    width = home.shape[1]
    rows, hidden = nodes * 2, len(pieces) * pieces[0].shape[1]
    scratch = [(nodes * 8, width)] + [(hidden, width)] * 3 + [(nodes * 8, width)]
    return pl.pallas_call(
        functools.partial(expert_ninth_kernel, nodes, len(pieces)),
        name="expert_ninth",
        out_shape=jax.ShapeDtypeStruct(home.shape, BF),
        in_specs=[WHOLE] * 3 + [ANY] * (len(pieces) + 1),
        out_specs=ANY,
        input_output_aliases={3 + len(pieces): 0},
        scratch_shapes=[pltpu.VMEM(s, BF) for s in scratch] + [pltpu.SemaphoreType.DMA((6,))],
        compiler_params=room(40),
        cost_estimate=expert_cost(rows, hidden, width),
    )(arrived_other, pair_out, pair_back, *pieces, home)


def expert_near(arrived, pieces, nodes):
    width = arrived.shape[1]
    rows, hidden = nodes * 8, len(pieces) * pieces[0].shape[1]
    return pl.pallas_call(
        functools.partial(expert_near_kernel, nodes, len(pieces)),
        name="expert_near",
        out_shape=tuple(jax.ShapeDtypeStruct((rows, width), t) for t in (F32, F32, BF, BF)),
        in_specs=[ANY] * (1 + len(pieces)),
        out_specs=(WHOLE,) * 4,
        scratch_shapes=[pltpu.VMEM((hidden, width), BF)] * 3 + [pltpu.SemaphoreType.DMA((6,))],
        compiler_params=room(46),
        cost_estimate=expert_cost(rows, hidden, width),
    )(arrived, *pieces)


def expert_far(near, pieces, nodes):
    out_part, back_part, xs, gs = near
    rows, width = xs.shape
    hidden = len(pieces) * pieces[0].shape[1]
    scratch = [((rows, width), F32)] * 2 + [((hidden, width), BF)] * 3 + [((rows, width), BF)] * 2
    return pl.pallas_call(
        functools.partial(expert_far_kernel, nodes, len(pieces)),
        name="expert_far",
        out_shape=jax.ShapeDtypeStruct((nodes * OUT1_ROWS, width), BF),
        in_specs=[WHOLE] * 2 + [ANY] * (2 + len(pieces)),
        out_specs=ANY,
        scratch_shapes=[pltpu.VMEM(s, t) for s, t in scratch] + [pltpu.SemaphoreType.DMA((8,))],
        compiler_params=room(61),
        cost_estimate=expert_cost(rows, hidden, width),
    )(on_chip(xs), on_chip(gs), out_part, back_part, *pieces)


def mixed(rows, places, values):
    ids = lax.broadcasted_iota(jnp.int32, (places.shape[0], rows.shape[0]), 1)
    total = jnp.zeros(ids.shape, F32)
    for k in range(TOP):
        total = total + jnp.where(places[:, k : k + 1] == ids, values[:, k : k + 1], 0.0)
    return jnp.dot(total.astype(BF), rows, preferred_element_type=F32)


def weight_grads(rows, grads, places):
    table = lax.dot_general(grads, rows, (((1,), (1,)), ((), ())), preferred_element_type=F32)
    ids = lax.broadcasted_iota(jnp.int32, table.shape, 1)
    lane = lax.broadcasted_iota(jnp.int32, (table.shape[0], 128), 1)
    result = jnp.zeros(lane.shape, F32)
    for k in range(TOP):
        column = jnp.sum(jnp.where(places[:, k : k + 1] == ids, table, 0.0), axis=1, keepdims=True)
        result = result + jnp.where(lane == k, column, 0.0)
    return result


def combine_pair_kernel(home, places_ref, values_ref, grads, grads_other, back, own, dw_other, dw_own):
    toks = grads.shape[0]
    rows = home[...]
    total = mixed(rows, places_ref[...], values_ref[...])
    back[...] = total[: 2 * toks].astype(BF)
    own[...] = total[2 * toks :]
    both = jnp.concatenate([grads_other[...], grads[...]], axis=0)
    heads = jnp.concatenate([places_ref[:toks], places_ref[2 * toks : 3 * toks]], axis=0)
    dw = weight_grads(rows, both, heads)
    dw_other[...] = jnp.transpose(dw[:toks])[:8]
    dw_own[...] = jnp.transpose(dw[toks:])[:8]


def combine_full_kernel(
    home, places_ref, values_ref, dw_own, dw_back, grads_at, own_at, returned_at, combined, d_tokens, d_weights, *scratch
):
    grads, own, returned, sems = scratch
    toks = grads.shape[0]
    copies = [
        pltpu.make_async_copy(src, dst, sems.at[i])
        for i, (src, dst) in enumerate(((own_at, own), (returned_at, returned), (grads_at, grads)))
    ]
    for copy in copies:
        copy.start()
    rows = home[...]
    total = mixed(rows, places_ref[...], values_ref[...])
    copies[0].wait()
    copies[1].wait()
    total = total + own[...] + returned[...].astype(F32)
    combined[...] = total[:toks].astype(BF)
    d_tokens[...] = total[toks:].astype(BF)
    copies[2].wait()
    dw = jnp.transpose(weight_grads(rows, grads[...], places_ref[:toks]))[:8] + dw_own[...] + dw_back[...]
    d_weights[...] = dw[:TOP]


def combine_pair(home, places, values, grads, grads_other):
    toks, width = grads.shape
    return pl.pallas_call(
        combine_pair_kernel,
        name="combine_pair",
        out_shape=(
            jax.ShapeDtypeStruct((2 * toks, width), BF),
            jax.ShapeDtypeStruct((2 * toks, width), F32),
            jax.ShapeDtypeStruct((8, toks), F32),
            jax.ShapeDtypeStruct((8, toks), F32),
        ),
        compiler_params=room(60),
        cost_estimate=pl.CostEstimate(
            flops=12 * toks * home.shape[0] * width, transcendentals=0, bytes_accessed=12 * 1024 * 1024
        ),
    )(home, places, values, grads, grads_other)


def combine_full(home, places, values, grads, own, returned, dw_own, dw_back):
    toks, width = grads.shape
    return pl.pallas_call(
        combine_full_kernel,
        name="combine_full",
        out_shape=(
            jax.ShapeDtypeStruct((toks, width), BF),
            jax.ShapeDtypeStruct((toks, width), BF),
            jax.ShapeDtypeStruct((TOP, toks), F32),
        ),
        in_specs=[WHOLE] * 5 + [ANY] * 3,
        out_specs=(WHOLE,) * 3,
        scratch_shapes=[
            pltpu.VMEM((toks, width), BF),
            pltpu.VMEM((2 * toks, width), F32),
            pltpu.VMEM((2 * toks, width), BF),
            pltpu.SemaphoreType.DMA((3,)),
        ],
        compiler_params=room(57),
        cost_estimate=pl.CostEstimate(
            flops=6 * toks * home.shape[0] * width, transcendentals=0, bytes_accessed=8 * 1024 * 1024
        ),
    )(on_chip(home), places, values, dw_own, dw_back, grads, own, returned)


def shards(tokens, route, combine_weights, w_gate, w_up, w_down, grad_out):
    nodes = lax.axis_size("node")
    planes = lax.axis_size("local")
    toks, _ = tokens.shape
    up = [(i, (i + 1) % planes) for i in range(planes)]
    down = [(i, (i - 1) % planes) for i in range(planes)]
    across = [(i, (i + 2) % planes) for i in range(planes)]

    def send(value, pairs):
        return lax.ppermute(value, "local", pairs)

    def exchange(rows):
        return lax.all_to_all(rows, "node", split_axis=0, concat_axis=0, tiled=True)

    tokens_other, grads_other = send(tokens, across), send(grad_out, across)
    route_t = route.T
    weight_t = combine_weights.T
    small = send(jnp.concatenate([weight_t, route_t.astype(F32)], axis=0), across)
    weight_other = small[:TOP]
    route_other = small[TOP:].astype(jnp.int32)

    gate_t = jnp.swapaxes(w_gate, 1, 2)
    up_t = jnp.swapaxes(w_up, 1, 2)
    half = gate_t.shape[1] // 2

    def piece(expert, part):
        cut = slice(part * half, (part + 1) * half)
        return jnp.stack([gate_t[expert, cut], up_t[expert, cut], w_down[expert, cut]])

    p0a, p0b, p1a, p1b = piece(0, 0), piece(0, 1), piece(1, 0), piece(1, 1)
    w0 = [p0a, p0b, send(p0a, down), send(p0b, up)]
    below_b, above_a = send(p1b, up), send(p1a, down)
    below_a, above_b = send(p1a, up), send(p1b, down)
    pair1 = [p1a, p1b, below_b, above_a]
    near1 = pair1 + [below_a, above_b]
    far1 = [send(p1a, across), send(p1b, across)]

    slot_own, slot_other = slots_of(route_t), slots_of(route_other)

    own_rows = dispatch(dispatch_own_kernel, nodes * OWN_ROWS, route_t, tokens, grad_out)
    arrived = exchange(own_rows)
    other_rows = dispatch(
        dispatch_other_kernel,
        nodes * OTHER_ROWS,
        route_t,
        route_other,
        tokens,
        grad_out,
        tokens_other,
        grads_other,
    )
    arrived_other = exchange(other_rows)

    arrived_other = on_chip(arrived_other)
    pair_rows = expert_pair(arrived, arrived_other, w0, nodes)
    rows0 = expert_ninth(arrived_other, pair_rows, pair1, nodes)
    home0 = exchange(rows0)
    near = expert_near(arrived, near1, nodes)
    rows1 = expert_far(near, far1, nodes)
    home1 = exchange(rows1)

    def pair_place(route_rows, slot, main, rest):
        odd = route_rows % 2
        ninth = slot == 8
        index = jnp.where(ninth, rest + 4 * odd, main + slot)
        return jnp.where((odd == 0) | ninth, (route_rows // 2) * OUT0_ROWS + index, -1)

    def home_place(main, rest):
        return pair_place(route_t, slot_own, main, rest)

    def other_place(main, rest):
        return pair_place(route_other, slot_other, main, rest)

    def full_place(main):
        kept = (route_t % 2 == 1) & (slot_own < 8)
        return jnp.where(kept, (route_t // 2) * OUT1_ROWS + main + slot_own, -1)

    def stacked(*parts):
        return jnp.concatenate([p.T for p in parts], axis=0)

    places0 = stacked(other_place(8, 33), other_place(24, 35), home_place(0, 32), home_place(16, 34))
    places1 = stacked(full_place(0), full_place(8))
    values0 = stacked(weight_other, weight_other, weight_t, weight_t)
    values1 = values0[2 * toks :]
    back, kept, dw_other, dw_own = combine_pair(home0, places0, values0, grad_out, grads_other)
    returned = send(back, across)
    dw_back = send(dw_other, across)
    combined, d_tokens, d_weights_t = combine_full(
        home1, places1, values1, grad_out, kept, returned, dw_own, dw_back
    )
    return combined, d_tokens, d_weights_t.T


def solution(mesh):
    tokens_spec = P(("node", "local"), None)

    return jax.shard_map(
        shards,
        mesh=mesh,
        in_specs=(
            tokens_spec,
            tokens_spec,
            tokens_spec,
            P("node", None, "local"),
            P("node", None, "local"),
            P("node", "local", None),
            tokens_spec,
        ),
        out_specs=(tokens_spec, tokens_spec, tokens_spec),
        check_vma=False,
    )
```

```python
import functools

import jax
import jax.numpy as jnp
from jax import lax
from jax.experimental import pallas as pl
from jax.experimental.pallas import tpu as pltpu
from jax.sharding import PartitionSpec as P

EXPERTS = 64
TOP = 4
BF = jnp.bfloat16
F32 = jnp.float32

OWN_ROWS = 32
OTHER_ROWS = 24
OUT0_ROWS = 40
OUT1_ROWS = 16


def slots_of(route_t):
    toks = route_t.shape[1]
    expert_ids = lax.broadcasted_iota(jnp.int32, (EXPERTS, toks), 0)
    hits = [(route_t[k : k + 1] == expert_ids) for k in range(TOP)]
    named = sum(jnp.where(h, 1.0, 0.0) for h in hits).astype(BF)
    from_ids = lax.broadcasted_iota(jnp.int32, (toks, toks), 0)
    to_ids = lax.broadcasted_iota(jnp.int32, (toks, toks), 1)
    before = jnp.where(from_ids < to_ids, 1.0, 0.0).astype(BF)
    earlier = jnp.dot(named, before, preferred_element_type=F32)
    slots = [jnp.sum(jnp.where(h, earlier, 0.0), axis=0, keepdims=True) for h in hits]
    return jnp.concatenate(slots, axis=0).astype(jnp.int32)


def dispatch_rows(pairs, block, first):
    total = None
    for places, values in pairs:
        ids = lax.broadcasted_iota(jnp.int32, (block, places.shape[1]), 0) + first
        hot = jnp.zeros(ids.shape, F32)
        for k in range(TOP):
            hot = hot + jnp.where(places[k : k + 1] == ids, 1.0, 0.0)
        term = jnp.dot(hot.astype(BF), values, preferred_element_type=F32)
        total = term if total is None else total + term
    return total.astype(BF)


def dispatch_own_kernel(route_ref, tokens, grads, rows):
    block = rows.shape[0]
    first = pl.program_id(0) * block
    route = route_ref[...]
    slot = slots_of(route)
    base = (route // 2) * OWN_ROWS + (route % 2) * 16 + slot
    kept = slot < 8
    x_place, g_place = jnp.where(kept, base, -1), jnp.where(kept, base + 8, -1)
    rows[...] = dispatch_rows([(x_place, tokens[...]), (g_place, grads[...])], block, first)


def dispatch_other_kernel(route_ref, route_other_ref, tokens, grads, tokens_other, grads_other, rows):
    block = rows.shape[0]
    first = pl.program_id(0) * block
    route = route_ref[...]
    odd = route % 2
    ninth = slots_of(route) == 8
    base = (route // 2) * OTHER_ROWS
    x_place = jnp.where(ninth, base + 16 + 4 * odd, -1)
    g_place = jnp.where(ninth, base + 18 + 4 * odd, -1)
    route = route_other_ref[...]
    odd = route % 2
    slot = slots_of(route)
    ninth = slot == 8
    base = (route // 2) * OTHER_ROWS
    kept = (odd == 0) | ninth
    x_far = jnp.where(kept, base + jnp.where(ninth, 17 + 4 * odd, slot), -1)
    g_far = jnp.where(kept, base + jnp.where(ninth, 19 + 4 * odd, slot + 8), -1)
    rows[...] = dispatch_rows(
        [(x_place, tokens[...]), (g_place, grads[...]), (x_far, tokens_other[...]), (g_far, grads_other[...])],
        block,
        first,
    )


def dispatch(kernel, rows, *args):
    width = args[-1].shape[1]
    steps = 4

    def whole(x):
        return pl.BlockSpec(x.shape, lambda i: (0, 0))

    return pl.pallas_call(
        kernel,
        grid=(steps,),
        out_shape=jax.ShapeDtypeStruct((rows, width), BF),
        in_specs=[whole(x) for x in args],
        out_specs=pl.BlockSpec((rows // steps, width), lambda i: (i, 0)),
        cost_estimate=pl.CostEstimate(
            flops=4 * rows * 128 * width, transcendentals=0, bytes_accessed=4 * rows * width
        ),
    )(*args)


def landed(dst, sem):
    pltpu.make_async_copy(dst, dst, sem).wait()


def fetch_rows(nodes, src, stride, first, dst, at, sem):
    def step(n, carry):
        frm = src.at[pl.ds(pl.multiple_of(n * stride + first, 8), 8)]
        to = dst.at[pl.ds(pl.multiple_of(at + n * 8, 8), 8)]
        pltpu.make_async_copy(frm, to, sem).start()
        return carry

    lax.fori_loop(0, nodes, step, 0)


def put_rows(nodes, src, at, dst, stride, first, sem):
    def step(n, carry):
        frm = src.at[pl.ds(pl.multiple_of(at + n * 8, 8), 8)]
        to = dst.at[pl.ds(pl.multiple_of(n * stride + first, 8), 8)]
        pltpu.make_async_copy(frm, to, sem).start()
        return carry

    lax.fori_loop(0, nodes, step, 0)


def fetch_weights(pieces, weights, sems, first):
    part = pieces[0].shape[1]
    for j, w in enumerate(weights):
        for i, p in enumerate(pieces):
            pltpu.make_async_copy(p.at[j], w.at[pl.ds(i * part, part)], sems.at[first + j]).start()


def picked(nodes, extra, offset, out_major):
    shape = (nodes * 8, nodes * extra) if out_major else (nodes * extra, nodes * 8)
    compact = lax.broadcasted_iota(jnp.int32, shape, 1 if out_major else 0)
    wide = lax.broadcasted_iota(jnp.int32, shape, 0 if out_major else 1)
    want = (compact // extra) * 8 + offset + compact % extra
    return (want == wide).astype(F32).astype(BF)


def by_hidden(rows, w):
    return lax.dot_general(rows, w, (((1,), (1,)), ((), ())), preferred_element_type=F32)


def by_row(rows, w):
    return jnp.dot(rows, w, preferred_element_type=F32)


def inner(x, g, wg, wu, wd):
    gate = by_hidden(x, wg)
    upper = by_hidden(x, wu)
    d_hidden = by_hidden(g, wd)
    s = jax.nn.sigmoid(gate)
    act = gate * s
    hidden = (act * upper).astype(BF)
    d_gate = (d_hidden * upper * s * (1.0 + gate * (1.0 - s))).astype(BF)
    d_up = (d_hidden * act).astype(BF)
    return hidden, d_gate, d_up


def expert_pair_kernel(nodes, n_pieces, *refs):
    arrived, arrived_other, pieces = refs[0], refs[1], refs[2 : 2 + n_pieces]
    home, ninth_out, ninth_back = refs[2 + n_pieces : 5 + n_pieces]
    xs, gs, rest, wg, wu, wd, outs, backs, sems = refs[5 + n_pieces :]
    main, small = nodes * 16, nodes * 2
    fetch_rows(nodes, arrived, OWN_ROWS, 0, xs, 0, sems.at[0])
    fetch_rows(nodes, arrived_other, OTHER_ROWS, 0, xs, nodes * 8, sems.at[0])
    fetch_rows(nodes, arrived_other, OTHER_ROWS, 16, rest, 0, sems.at[1])
    fetch_weights(pieces, (wg, wu, wd), sems, 3)
    fetch_rows(nodes, arrived, OWN_ROWS, 8, gs, 0, sems.at[2])
    fetch_rows(nodes, arrived_other, OTHER_ROWS, 8, gs, nodes * 8, sems.at[2])
    landed(rest, sems.at[1])
    xs[pl.ds(main, small)] = by_row(picked(nodes, 2, 0, False), rest[...]).astype(BF)
    gs[pl.ds(main, small)] = by_row(picked(nodes, 2, 2, False), rest[...]).astype(BF)
    landed(xs.at[pl.ds(0, main)], sems.at[0])
    landed(wg, sems.at[3])
    landed(wu, sems.at[4])
    landed(gs.at[pl.ds(0, main)], sems.at[2])
    landed(wd, sems.at[5])
    size = (main + small) // 2

    def block(b, carry):
        at = pl.ds(pl.multiple_of(b * size, 16), size)
        hidden, d_gate, d_up = inner(xs[at], gs[at], wg[...], wu[...], wd[...])
        outs[at] = by_row(hidden, wd[...]).astype(BF)
        backs[at] = (by_row(d_gate, wg[...]) + by_row(d_up, wu[...])).astype(BF)
        return carry

    lax.fori_loop(0, 2, block, 0)
    put_rows(nodes, outs, 0, home, OUT0_ROWS, 0, sems.at[0])
    put_rows(nodes, outs, nodes * 8, home, OUT0_ROWS, 8, sems.at[0])
    put_rows(nodes, backs, 0, home, OUT0_ROWS, 16, sems.at[1])
    put_rows(nodes, backs, nodes * 8, home, OUT0_ROWS, 24, sems.at[1])
    ninth_out[...] = outs[pl.ds(main, small)]
    ninth_back[...] = backs[pl.ds(main, small)]
    landed(outs.at[pl.ds(0, main)], sems.at[0])
    landed(backs.at[pl.ds(0, main)], sems.at[1])


def expert_ninth_kernel(nodes, n_pieces, *refs):
    arrived_other, pair_out, pair_back, pieces = refs[0], refs[1], refs[2], refs[3 : 3 + n_pieces]
    home = refs[4 + n_pieces]
    rest, wg, wu, wd, out_rest, sems = refs[5 + n_pieces :]
    fetch_rows(nodes, arrived_other, OTHER_ROWS, 16, rest, 0, sems.at[1])
    fetch_weights(pieces, (wg, wu, wd), sems, 3)
    landed(rest, sems.at[1])
    xs = by_row(picked(nodes, 2, 4, False), rest[...]).astype(BF)
    gs = by_row(picked(nodes, 2, 6, False), rest[...]).astype(BF)
    carried = by_row(picked(nodes, 2, 0, True), pair_out[...]) + by_row(picked(nodes, 2, 2, True), pair_back[...])
    landed(wg, sems.at[3])
    landed(wu, sems.at[4])
    landed(wd, sems.at[5])
    hidden, d_gate, d_up = inner(xs, gs, wg[...], wu[...], wd[...])
    out = by_row(hidden, wd[...]).astype(BF)
    back = (by_row(d_gate, wg[...]) + by_row(d_up, wu[...])).astype(BF)
    out_rest[...] = (
        carried + by_row(picked(nodes, 2, 4, True), out) + by_row(picked(nodes, 2, 6, True), back)
    ).astype(BF)
    put_rows(nodes, out_rest, 0, home, OUT0_ROWS, 32, sems.at[2])
    landed(out_rest, sems.at[2])


def expert_near_kernel(nodes, n_pieces, *refs):
    arrived, pieces = refs[0], refs[1 : 1 + n_pieces]
    out_part, back_part, xs, gs = refs[1 + n_pieces : 5 + n_pieces]
    wg, wu, wd, sems = refs[5 + n_pieces :]
    fetch_rows(nodes, arrived, OWN_ROWS, 16, xs, 0, sems.at[0])
    fetch_rows(nodes, arrived, OWN_ROWS, 24, gs, 0, sems.at[2])
    fetch_weights(pieces, (wg, wu, wd), sems, 3)
    landed(xs, sems.at[0])
    landed(gs, sems.at[2])
    landed(wg, sems.at[3])
    landed(wu, sems.at[4])
    landed(wd, sems.at[5])
    size = nodes * 4

    def block(b, carry):
        at = pl.ds(pl.multiple_of(b * size, 16), size)
        hidden, d_gate, d_up = inner(xs[at], gs[at], wg[...], wu[...], wd[...])
        out_part[at] = by_row(hidden, wd[...])
        back_part[at] = by_row(d_gate, wg[...]) + by_row(d_up, wu[...])
        return carry

    lax.fori_loop(0, 2, block, 0)


def expert_far_kernel(nodes, n_pieces, *refs):
    xs, gs, out_at, back_at = refs[:4]
    pieces, home = refs[4 : 4 + n_pieces], refs[4 + n_pieces]
    out_part, back_part, wg, wu, wd, outs, backs, sems = refs[5 + n_pieces :]
    fetch_weights(pieces, (wg, wu, wd), sems, 3)
    pltpu.make_async_copy(out_at, out_part, sems.at[6]).start()
    pltpu.make_async_copy(back_at, back_part, sems.at[7]).start()
    landed(wg, sems.at[3])
    landed(wu, sems.at[4])
    landed(wd, sems.at[5])
    hidden, d_gate, d_up = inner(xs[...], gs[...], wg[...], wu[...], wd[...])
    landed(out_part, sems.at[6])
    outs[...] = (by_row(hidden, wd[...]) + out_part[...]).astype(BF)
    put_rows(nodes, outs, 0, home, OUT1_ROWS, 0, sems.at[0])
    landed(back_part, sems.at[7])
    backs[...] = (by_row(d_gate, wg[...]) + by_row(d_up, wu[...]) + back_part[...]).astype(BF)
    put_rows(nodes, backs, 0, home, OUT1_ROWS, 8, sems.at[1])
    landed(outs, sems.at[0])
    landed(backs, sems.at[1])


def on_chip(value):
    return pltpu.with_memory_space_constraint(value, pltpu.VMEM)


ANY = pl.BlockSpec(memory_space=pltpu.HBM)
WHOLE = pl.BlockSpec(memory_space=pltpu.VMEM)


def room(mib):
    return pltpu.CompilerParams(vmem_limit_bytes=mib * 1024 * 1024)


def expert_cost(rows, hidden, width):
    return pl.CostEstimate(
        flops=12 * rows * hidden * width,
        transcendentals=rows * hidden,
        bytes_accessed=2 * width * (4 * rows + 3 * hidden),
    )


def expert_pair(arrived, arrived_other, pieces, nodes):
    width = arrived.shape[1]
    rows, hidden = nodes * 18, len(pieces) * pieces[0].shape[1]
    ninth = jax.ShapeDtypeStruct((nodes * 2, width), BF)
    scratch = [(rows, width), (rows, width), (nodes * 8, width)] + [(hidden, width)] * 3
    scratch += [(rows, width), (rows, width)]
    return pl.pallas_call(
        functools.partial(expert_pair_kernel, nodes, len(pieces)),
        name="expert_pair",
        out_shape=(jax.ShapeDtypeStruct((nodes * OUT0_ROWS, width), BF), ninth, ninth),
        in_specs=[ANY, WHOLE] + [ANY] * len(pieces),
        out_specs=(ANY, WHOLE, WHOLE),
        scratch_shapes=[pltpu.VMEM(s, BF) for s in scratch] + [pltpu.SemaphoreType.DMA((6,))],
        compiler_params=room(46),
        cost_estimate=expert_cost(rows, hidden, width),
    )(arrived, arrived_other, *pieces)


def expert_ninth(arrived_other, pair_rows, pieces, nodes):
    home, pair_out, pair_back = pair_rows
    width = home.shape[1]
    rows, hidden = nodes * 2, len(pieces) * pieces[0].shape[1]
    scratch = [(nodes * 8, width)] + [(hidden, width)] * 3 + [(nodes * 8, width)]
    return pl.pallas_call(
        functools.partial(expert_ninth_kernel, nodes, len(pieces)),
        name="expert_ninth",
        out_shape=jax.ShapeDtypeStruct(home.shape, BF),
        in_specs=[WHOLE] * 3 + [ANY] * (len(pieces) + 1),
        out_specs=ANY,
        input_output_aliases={3 + len(pieces): 0},
        scratch_shapes=[pltpu.VMEM(s, BF) for s in scratch] + [pltpu.SemaphoreType.DMA((6,))],
        compiler_params=room(40),
        cost_estimate=expert_cost(rows, hidden, width),
    )(arrived_other, pair_out, pair_back, *pieces, home)


def expert_near(arrived, pieces, nodes):
    width = arrived.shape[1]
    rows, hidden = nodes * 8, len(pieces) * pieces[0].shape[1]
    return pl.pallas_call(
        functools.partial(expert_near_kernel, nodes, len(pieces)),
        name="expert_near",
        out_shape=tuple(jax.ShapeDtypeStruct((rows, width), t) for t in (F32, F32, BF, BF)),
        in_specs=[ANY] * (1 + len(pieces)),
        out_specs=(WHOLE,) * 4,
        scratch_shapes=[pltpu.VMEM((hidden, width), BF)] * 3 + [pltpu.SemaphoreType.DMA((6,))],
        compiler_params=room(46),
        cost_estimate=expert_cost(rows, hidden, width),
    )(arrived, *pieces)


def expert_far(near, pieces, nodes):
    out_part, back_part, xs, gs = near
    rows, width = xs.shape
    hidden = len(pieces) * pieces[0].shape[1]
    scratch = [((rows, width), F32)] * 2 + [((hidden, width), BF)] * 3 + [((rows, width), BF)] * 2
    return pl.pallas_call(
        functools.partial(expert_far_kernel, nodes, len(pieces)),
        name="expert_far",
        out_shape=jax.ShapeDtypeStruct((nodes * OUT1_ROWS, width), BF),
        in_specs=[WHOLE] * 2 + [ANY] * (2 + len(pieces)),
        out_specs=ANY,
        scratch_shapes=[pltpu.VMEM(s, t) for s, t in scratch] + [pltpu.SemaphoreType.DMA((8,))],
        compiler_params=room(61),
        cost_estimate=expert_cost(rows, hidden, width),
    )(on_chip(xs), on_chip(gs), out_part, back_part, *pieces)


def weighted_hot(places, values, rows):
    ids = lax.broadcasted_iota(jnp.int32, (places.shape[0], rows), 1)
    total = jnp.zeros(ids.shape, F32)
    for k in range(TOP):
        total = total + jnp.where(places[:, k : k + 1] == ids, values[:, k : k + 1], 0.0)
    return total.astype(BF)


def weight_grads(table, places):
    ids = lax.broadcasted_iota(jnp.int32, table.shape, 1)
    lane = lax.broadcasted_iota(jnp.int32, (table.shape[0], 128), 1)
    result = jnp.zeros(lane.shape, F32)
    for k in range(TOP):
        column = jnp.sum(jnp.where(places[:, k : k + 1] == ids, table, 0.0), axis=1, keepdims=True)
        result = result + jnp.where(lane == k, column, 0.0)
    return jnp.transpose(result)[:8]


COLUMNS = 512


def sweep(home, hot, grads, table, use):
    matrix = hot[...]
    table[...] = jnp.zeros_like(table)

    def block(c, carry):
        cols = pl.ds(pl.multiple_of(c * COLUMNS, COLUMNS), COLUMNS)
        rows = home[:, cols]
        use(cols, jnp.dot(matrix, rows, preferred_element_type=F32))
        part = by_hidden(grads[:, cols], rows)
        table[...] += part
        return carry

    lax.fori_loop(0, home.shape[1] // COLUMNS, block, 0)


def combine_pair_kernel(home, places, values, grads, mix, dw, hot, table):
    toks = grads.shape[0]
    hot[...] = weighted_hot(places[...], values[...], home.shape[0])

    def use(cols, total):
        mix[:, cols] = total.astype(mix.dtype)

    sweep(home, hot, grads, table, use)
    dw[...] = weight_grads(table[...], places[:toks])


def combine_full_kernel(
    home, places, values, dw_own, dw_back, grads_at, own_at, returned_at, combined, d_tokens, d_weights, *scratch
):
    grads, own, returned, hot, table, sems = scratch
    toks = grads.shape[0]
    copies = [
        pltpu.make_async_copy(src, dst, sems.at[i])
        for i, (src, dst) in enumerate(((own_at, own), (returned_at, returned), (grads_at, grads)))
    ]
    for copy in copies:
        copy.start()
    hot[...] = weighted_hot(places[...], values[...], home.shape[0])
    for copy in copies:
        copy.wait()

    def use(cols, total):
        total = total + own[:, cols] + returned[:, cols].astype(F32)
        combined[:, cols] = total[:toks].astype(BF)
        d_tokens[:, cols] = total[toks:].astype(BF)

    sweep(home, hot, grads, table, use)
    d_weights[...] = (weight_grads(table[...], places[:toks]) + dw_own[...] + dw_back[...])[:TOP]


def combine_pair(home, places, values, grads, kind):
    toks, width = grads.shape
    return pl.pallas_call(
        combine_pair_kernel,
        out_shape=(jax.ShapeDtypeStruct((2 * toks, width), kind), jax.ShapeDtypeStruct((8, toks), F32)),
        scratch_shapes=[pltpu.VMEM((2 * toks, home.shape[0]), BF), pltpu.VMEM((toks, home.shape[0]), F32)],
        compiler_params=room(60),
        cost_estimate=pl.CostEstimate(
            flops=6 * toks * home.shape[0] * width, transcendentals=0, bytes_accessed=8 * 1024 * 1024
        ),
    )(home, places, values, grads)


def combine_full(home, places, values, grads, own, returned, dw_own, dw_back):
    toks, width = grads.shape
    return pl.pallas_call(
        combine_full_kernel,
        name="combine_full",
        out_shape=(
            jax.ShapeDtypeStruct((toks, width), BF),
            jax.ShapeDtypeStruct((toks, width), BF),
            jax.ShapeDtypeStruct((TOP, toks), F32),
        ),
        in_specs=[WHOLE] * 5 + [ANY] * 3,
        out_specs=(WHOLE,) * 3,
        scratch_shapes=[
            pltpu.VMEM((toks, width), BF),
            pltpu.VMEM((2 * toks, width), F32),
            pltpu.VMEM((2 * toks, width), BF),
            pltpu.VMEM((2 * toks, home.shape[0]), BF),
            pltpu.VMEM((toks, home.shape[0]), F32),
            pltpu.SemaphoreType.DMA((3,)),
        ],
        compiler_params=room(57),
        cost_estimate=pl.CostEstimate(
            flops=6 * toks * home.shape[0] * width, transcendentals=0, bytes_accessed=8 * 1024 * 1024
        ),
    )(on_chip(home), places, values, dw_own, dw_back, grads, own, returned)


def shards(tokens, route, combine_weights, w_gate, w_up, w_down, grad_out):
    nodes = lax.axis_size("node")
    planes = lax.axis_size("local")
    up = [(i, (i + 1) % planes) for i in range(planes)]
    down = [(i, (i - 1) % planes) for i in range(planes)]
    across = [(i, (i + 2) % planes) for i in range(planes)]

    def send(value, pairs):
        return lax.ppermute(value, "local", pairs)

    def exchange(rows):
        return lax.all_to_all(rows, "node", split_axis=0, concat_axis=0, tiled=True)

    tokens_other, grads_other = send(tokens, across), send(grad_out, across)
    route_t = route.T
    weight_t = combine_weights.T
    small = send(jnp.concatenate([weight_t, route_t.astype(F32)], axis=0), across)
    weight_other = small[:TOP]
    route_other = small[TOP:].astype(jnp.int32)

    gate_t = jnp.swapaxes(w_gate, 1, 2)
    up_t = jnp.swapaxes(w_up, 1, 2)
    half = gate_t.shape[1] // 2

    def piece(expert, part):
        cut = slice(part * half, (part + 1) * half)
        return jnp.stack([gate_t[expert, cut], up_t[expert, cut], w_down[expert, cut]])

    p0a, p0b, p1a, p1b = piece(0, 0), piece(0, 1), piece(1, 0), piece(1, 1)
    w0 = [p0a, p0b, send(p0a, down), send(p0b, up)]
    below_b, above_a = send(p1b, up), send(p1a, down)
    below_a, above_b = send(p1a, up), send(p1b, down)
    pair1 = [p1a, p1b, below_b, above_a]
    near1 = pair1 + [below_a, above_b]
    far1 = [send(above_a, down), send(below_b, up)]

    slot_own, slot_other = slots_of(route_t), slots_of(route_other)

    own_rows = dispatch(dispatch_own_kernel, nodes * OWN_ROWS, route_t, tokens, grad_out)
    arrived = exchange(own_rows)
    other_rows = dispatch(
        dispatch_other_kernel,
        nodes * OTHER_ROWS,
        route_t,
        route_other,
        tokens,
        grad_out,
        tokens_other,
        grads_other,
    )
    arrived_other = exchange(other_rows)

    arrived_other = on_chip(arrived_other)
    pair_rows = expert_pair(arrived, arrived_other, w0, nodes)
    rows0 = expert_ninth(arrived_other, pair_rows, pair1, nodes)
    home0 = exchange(rows0)
    near = expert_near(arrived, near1, nodes)
    rows1 = expert_far(near, far1, nodes)
    home1 = exchange(rows1)

    def pair_place(route_rows, slot, main, rest):
        odd = route_rows % 2
        ninth = slot == 8
        index = jnp.where(ninth, rest + 4 * odd, main + slot)
        return jnp.where((odd == 0) | ninth, (route_rows // 2) * OUT0_ROWS + index, -1)

    def home_place(main, rest):
        return pair_place(route_t, slot_own, main, rest)

    def other_place(main, rest):
        return pair_place(route_other, slot_other, main, rest)

    def full_place(main):
        kept = (route_t % 2 == 1) & (slot_own < 8)
        return jnp.where(kept, (route_t // 2) * OUT1_ROWS + main + slot_own, -1)

    def stacked(*parts):
        return jnp.concatenate([p.T for p in parts], axis=0)

    places0 = stacked(home_place(0, 32), home_place(16, 34))
    places_other = stacked(other_place(8, 33), other_place(24, 35))
    places1 = stacked(full_place(0), full_place(8))
    values0, values_other = stacked(weight_t, weight_t), stacked(weight_other, weight_other)
    back, dw_other = combine_pair(home0, places_other, values_other, grads_other, BF)
    returned = send(back, across)
    dw_back = send(dw_other, across)
    kept, dw_own = combine_pair(home0, places0, values0, grad_out, F32)
    combined, d_tokens, d_weights_t = combine_full(
        home1, places1, values0, grad_out, kept, returned, dw_own, dw_back
    )
    return combined, d_tokens, d_weights_t.T


def solution(mesh):
    tokens_spec = P(("node", "local"), None)

    return jax.shard_map(
        shards,
        mesh=mesh,
        in_specs=(
            tokens_spec,
            tokens_spec,
            tokens_spec,
            P("node", None, "local"),
            P("node", None, "local"),
            P("node", "local", None),
            tokens_spec,
        ),
        out_specs=(tokens_spec, tokens_spec, tokens_spec),
        check_vma=False,
    )
```

```python
import functools

import jax
import jax.numpy as jnp
from jax import lax
from jax.experimental import pallas as pl
from jax.experimental.pallas import tpu as pltpu
from jax.sharding import PartitionSpec as P

EXPERTS = 64
TOP = 4
BF = jnp.bfloat16
F32 = jnp.float32

OWN_ROWS = 32
OTHER_ROWS = 24
OUT0_ROWS = 40
OUT1_ROWS = 16


def slots_of(route_t):
    toks = route_t.shape[1]
    expert_ids = lax.broadcasted_iota(jnp.int32, (EXPERTS, toks), 0)
    hits = [(route_t[k : k + 1] == expert_ids) for k in range(TOP)]
    named = sum(jnp.where(h, 1.0, 0.0) for h in hits).astype(BF)
    from_ids = lax.broadcasted_iota(jnp.int32, (toks, toks), 0)
    to_ids = lax.broadcasted_iota(jnp.int32, (toks, toks), 1)
    before = jnp.where(from_ids < to_ids, 1.0, 0.0).astype(BF)
    earlier = jnp.dot(named, before, preferred_element_type=F32)
    slots = [jnp.sum(jnp.where(h, earlier, 0.0), axis=0, keepdims=True) for h in hits]
    return jnp.concatenate(slots, axis=0).astype(jnp.int32)


def dispatch_rows(pairs, block, first):
    total = None
    for places, values in pairs:
        ids = lax.broadcasted_iota(jnp.int32, (block, places.shape[1]), 0) + first
        hot = jnp.zeros(ids.shape, F32)
        for k in range(TOP):
            hot = hot + jnp.where(places[k : k + 1] == ids, 1.0, 0.0)
        term = jnp.dot(hot.astype(BF), values, preferred_element_type=F32)
        total = term if total is None else total + term
    return total.astype(BF)


def dispatch_own_kernel(route_ref, tokens, grads, rows):
    block = rows.shape[0]
    first = pl.program_id(0) * block
    route = route_ref[...]
    slot = slots_of(route)
    base = (route // 2) * OWN_ROWS + (route % 2) * 16 + slot
    kept = slot < 8
    x_place, g_place = jnp.where(kept, base, -1), jnp.where(kept, base + 8, -1)
    rows[...] = dispatch_rows([(x_place, tokens[...]), (g_place, grads[...])], block, first)


def dispatch_other_kernel(route_ref, route_other_ref, tokens, grads, tokens_other, grads_other, rows):
    block = rows.shape[0]
    first = pl.program_id(0) * block
    route = route_ref[...]
    odd = route % 2
    ninth = slots_of(route) == 8
    base = (route // 2) * OTHER_ROWS
    x_place = jnp.where(ninth, base + 16 + 4 * odd, -1)
    g_place = jnp.where(ninth, base + 18 + 4 * odd, -1)
    route = route_other_ref[...]
    odd = route % 2
    slot = slots_of(route)
    ninth = slot == 8
    base = (route // 2) * OTHER_ROWS
    kept = (odd == 0) | ninth
    x_far = jnp.where(kept, base + jnp.where(ninth, 17 + 4 * odd, slot), -1)
    g_far = jnp.where(kept, base + jnp.where(ninth, 19 + 4 * odd, slot + 8), -1)
    rows[...] = dispatch_rows(
        [(x_place, tokens[...]), (g_place, grads[...]), (x_far, tokens_other[...]), (g_far, grads_other[...])],
        block,
        first,
    )


def dispatch(kernel, rows, *args):
    width = args[-1].shape[1]
    steps = 4

    def whole(x):
        return pl.BlockSpec(x.shape, lambda i: (0, 0))

    return pl.pallas_call(
        kernel,
        grid=(steps,),
        out_shape=jax.ShapeDtypeStruct((rows, width), BF),
        in_specs=[whole(x) for x in args],
        out_specs=pl.BlockSpec((rows // steps, width), lambda i: (i, 0)),
        cost_estimate=pl.CostEstimate(
            flops=4 * rows * 128 * width, transcendentals=0, bytes_accessed=4 * rows * width
        ),
    )(*args)


def landed(dst, sem):
    pltpu.make_async_copy(dst, dst, sem).wait()


def fetch_rows(nodes, src, stride, first, dst, at, sem):
    def step(n, carry):
        frm = src.at[pl.ds(pl.multiple_of(n * stride + first, 8), 8)]
        to = dst.at[pl.ds(pl.multiple_of(at + n * 8, 8), 8)]
        pltpu.make_async_copy(frm, to, sem).start()
        return carry

    lax.fori_loop(0, nodes, step, 0)


def put_rows(nodes, src, at, dst, stride, first, sem):
    def step(n, carry):
        frm = src.at[pl.ds(pl.multiple_of(at + n * 8, 8), 8)]
        to = dst.at[pl.ds(pl.multiple_of(n * stride + first, 8), 8)]
        pltpu.make_async_copy(frm, to, sem).start()
        return carry

    lax.fori_loop(0, nodes, step, 0)


def fetch_weights(pieces, weights, sems, first):
    part = pieces[0].shape[1]
    for j, w in enumerate(weights):
        for i, p in enumerate(pieces):
            pltpu.make_async_copy(p.at[j], w.at[pl.ds(i * part, part)], sems.at[first + j]).start()


def picked(nodes, extra, offset, out_major):
    shape = (nodes * 8, nodes * extra) if out_major else (nodes * extra, nodes * 8)
    compact = lax.broadcasted_iota(jnp.int32, shape, 1 if out_major else 0)
    wide = lax.broadcasted_iota(jnp.int32, shape, 0 if out_major else 1)
    want = (compact // extra) * 8 + offset + compact % extra
    return (want == wide).astype(F32).astype(BF)


def by_hidden(rows, w):
    return lax.dot_general(rows, w, (((1,), (1,)), ((), ())), preferred_element_type=F32)


def by_row(rows, w):
    return jnp.dot(rows, w, preferred_element_type=F32)


def inner(x, g, wg, wu, wd):
    gate = by_hidden(x, wg)
    upper = by_hidden(x, wu)
    d_hidden = by_hidden(g, wd)
    s = jax.nn.sigmoid(gate)
    act = gate * s
    hidden = (act * upper).astype(BF)
    d_gate = (d_hidden * upper * s * (1.0 + gate * (1.0 - s))).astype(BF)
    d_up = (d_hidden * act).astype(BF)
    return hidden, d_gate, d_up


def expert_pair_kernel(nodes, n_pieces, *refs):
    arrived, arrived_other, pieces = refs[0], refs[1], refs[2 : 2 + n_pieces]
    home, ninth_out, ninth_back = refs[2 + n_pieces : 5 + n_pieces]
    xs, gs, rest, wg, wu, wd, outs, backs, sems = refs[5 + n_pieces :]
    main, small = nodes * 16, nodes * 2
    fetch_rows(nodes, arrived, OWN_ROWS, 0, xs, 0, sems.at[0])
    fetch_rows(nodes, arrived_other, OTHER_ROWS, 0, xs, nodes * 8, sems.at[0])
    fetch_rows(nodes, arrived_other, OTHER_ROWS, 16, rest, 0, sems.at[1])
    fetch_weights(pieces, (wg, wu, wd), sems, 3)
    fetch_rows(nodes, arrived, OWN_ROWS, 8, gs, 0, sems.at[2])
    fetch_rows(nodes, arrived_other, OTHER_ROWS, 8, gs, nodes * 8, sems.at[2])
    landed(rest, sems.at[1])
    xs[pl.ds(main, small)] = by_row(picked(nodes, 2, 0, False), rest[...]).astype(BF)
    gs[pl.ds(main, small)] = by_row(picked(nodes, 2, 2, False), rest[...]).astype(BF)
    landed(xs.at[pl.ds(0, main)], sems.at[0])
    landed(wg, sems.at[3])
    landed(wu, sems.at[4])
    landed(gs.at[pl.ds(0, main)], sems.at[2])
    landed(wd, sems.at[5])
    size = (main + small) // 2

    def block(b, carry):
        at = pl.ds(pl.multiple_of(b * size, 16), size)
        hidden, d_gate, d_up = inner(xs[at], gs[at], wg[...], wu[...], wd[...])
        outs[at] = by_row(hidden, wd[...]).astype(BF)
        backs[at] = (by_row(d_gate, wg[...]) + by_row(d_up, wu[...])).astype(BF)
        return carry

    lax.fori_loop(0, 2, block, 0)
    put_rows(nodes, outs, 0, home, OUT0_ROWS, 0, sems.at[0])
    put_rows(nodes, outs, nodes * 8, home, OUT0_ROWS, 8, sems.at[0])
    put_rows(nodes, backs, 0, home, OUT0_ROWS, 16, sems.at[1])
    put_rows(nodes, backs, nodes * 8, home, OUT0_ROWS, 24, sems.at[1])
    ninth_out[...] = outs[pl.ds(main, small)]
    ninth_back[...] = backs[pl.ds(main, small)]
    landed(outs.at[pl.ds(0, main)], sems.at[0])
    landed(backs.at[pl.ds(0, main)], sems.at[1])


def expert_ninth_kernel(nodes, n_pieces, *refs):
    arrived_other, pair_out, pair_back, pieces = refs[0], refs[1], refs[2], refs[3 : 3 + n_pieces]
    home = refs[4 + n_pieces]
    rest, wg, wu, wd, out_rest, sems = refs[5 + n_pieces :]
    fetch_rows(nodes, arrived_other, OTHER_ROWS, 16, rest, 0, sems.at[1])
    fetch_weights(pieces, (wg, wu, wd), sems, 3)
    landed(rest, sems.at[1])
    xs = by_row(picked(nodes, 2, 4, False), rest[...]).astype(BF)
    gs = by_row(picked(nodes, 2, 6, False), rest[...]).astype(BF)
    carried = by_row(picked(nodes, 2, 0, True), pair_out[...]) + by_row(picked(nodes, 2, 2, True), pair_back[...])
    landed(wg, sems.at[3])
    landed(wu, sems.at[4])
    landed(wd, sems.at[5])
    hidden, d_gate, d_up = inner(xs, gs, wg[...], wu[...], wd[...])
    out = by_row(hidden, wd[...]).astype(BF)
    back = (by_row(d_gate, wg[...]) + by_row(d_up, wu[...])).astype(BF)
    out_rest[...] = (
        carried + by_row(picked(nodes, 2, 4, True), out) + by_row(picked(nodes, 2, 6, True), back)
    ).astype(BF)
    put_rows(nodes, out_rest, 0, home, OUT0_ROWS, 32, sems.at[2])
    landed(out_rest, sems.at[2])


def expert_near_kernel(nodes, n_pieces, *refs):
    arrived, pieces = refs[0], refs[1 : 1 + n_pieces]
    out_part, back_part, xs, gs = refs[1 + n_pieces : 5 + n_pieces]
    wg, wu, wd, sems = refs[5 + n_pieces :]
    fetch_rows(nodes, arrived, OWN_ROWS, 16, xs, 0, sems.at[0])
    fetch_rows(nodes, arrived, OWN_ROWS, 24, gs, 0, sems.at[2])
    fetch_weights(pieces, (wg, wu, wd), sems, 3)
    landed(xs, sems.at[0])
    landed(gs, sems.at[2])
    landed(wg, sems.at[3])
    landed(wu, sems.at[4])
    landed(wd, sems.at[5])
    size = nodes * 4

    def block(b, carry):
        at = pl.ds(pl.multiple_of(b * size, 16), size)
        hidden, d_gate, d_up = inner(xs[at], gs[at], wg[...], wu[...], wd[...])
        out_part[at] = by_row(hidden, wd[...])
        back_part[at] = by_row(d_gate, wg[...]) + by_row(d_up, wu[...])
        return carry

    lax.fori_loop(0, 2, block, 0)


def expert_far_kernel(nodes, n_pieces, *refs):
    xs, gs, out_at, back_at = refs[:4]
    pieces, home = refs[4 : 4 + n_pieces], refs[4 + n_pieces]
    out_part, back_part, wg, wu, wd, outs, backs, sems = refs[5 + n_pieces :]
    fetch_weights(pieces, (wg, wu, wd), sems, 3)
    pltpu.make_async_copy(out_at, out_part, sems.at[6]).start()
    pltpu.make_async_copy(back_at, back_part, sems.at[7]).start()
    landed(wg, sems.at[3])
    landed(wu, sems.at[4])
    landed(wd, sems.at[5])
    hidden, d_gate, d_up = inner(xs[...], gs[...], wg[...], wu[...], wd[...])
    landed(out_part, sems.at[6])
    outs[...] = (by_row(hidden, wd[...]) + out_part[...]).astype(BF)
    put_rows(nodes, outs, 0, home, OUT1_ROWS, 0, sems.at[0])
    landed(back_part, sems.at[7])
    backs[...] = (by_row(d_gate, wg[...]) + by_row(d_up, wu[...]) + back_part[...]).astype(BF)
    put_rows(nodes, backs, 0, home, OUT1_ROWS, 8, sems.at[1])
    landed(outs, sems.at[0])
    landed(backs, sems.at[1])


def on_chip(value):
    return pltpu.with_memory_space_constraint(value, pltpu.VMEM)


ANY = pl.BlockSpec(memory_space=pltpu.HBM)
WHOLE = pl.BlockSpec(memory_space=pltpu.VMEM)


def room(mib):
    return pltpu.CompilerParams(vmem_limit_bytes=mib * 1024 * 1024)


def expert_cost(rows, hidden, width):
    return pl.CostEstimate(
        flops=12 * rows * hidden * width,
        transcendentals=rows * hidden,
        bytes_accessed=2 * width * (4 * rows + 3 * hidden),
    )


def expert_pair(arrived, arrived_other, pieces, nodes):
    width = arrived.shape[1]
    rows, hidden = nodes * 18, len(pieces) * pieces[0].shape[1]
    ninth = jax.ShapeDtypeStruct((nodes * 2, width), BF)
    scratch = [(rows, width), (rows, width), (nodes * 8, width)] + [(hidden, width)] * 3
    scratch += [(rows, width), (rows, width)]
    return pl.pallas_call(
        functools.partial(expert_pair_kernel, nodes, len(pieces)),
        name="expert_pair",
        out_shape=(jax.ShapeDtypeStruct((nodes * OUT0_ROWS, width), BF), ninth, ninth),
        in_specs=[ANY, WHOLE] + [ANY] * len(pieces),
        out_specs=(ANY, WHOLE, WHOLE),
        scratch_shapes=[pltpu.VMEM(s, BF) for s in scratch] + [pltpu.SemaphoreType.DMA((6,))],
        compiler_params=room(46),
        cost_estimate=expert_cost(rows, hidden, width),
    )(arrived, arrived_other, *pieces)


def expert_ninth(arrived_other, pair_rows, pieces, nodes):
    home, pair_out, pair_back = pair_rows
    width = home.shape[1]
    rows, hidden = nodes * 2, len(pieces) * pieces[0].shape[1]
    scratch = [(nodes * 8, width)] + [(hidden, width)] * 3 + [(nodes * 8, width)]
    return pl.pallas_call(
        functools.partial(expert_ninth_kernel, nodes, len(pieces)),
        name="expert_ninth",
        out_shape=jax.ShapeDtypeStruct(home.shape, BF),
        in_specs=[WHOLE] * 3 + [ANY] * (len(pieces) + 1),
        out_specs=ANY,
        input_output_aliases={3 + len(pieces): 0},
        scratch_shapes=[pltpu.VMEM(s, BF) for s in scratch] + [pltpu.SemaphoreType.DMA((6,))],
        compiler_params=room(40),
        cost_estimate=expert_cost(rows, hidden, width),
    )(arrived_other, pair_out, pair_back, *pieces, home)


def expert_near(arrived, pieces, nodes):
    width = arrived.shape[1]
    rows, hidden = nodes * 8, len(pieces) * pieces[0].shape[1]
    return pl.pallas_call(
        functools.partial(expert_near_kernel, nodes, len(pieces)),
        name="expert_near",
        out_shape=tuple(jax.ShapeDtypeStruct((rows, width), t) for t in (F32, F32, BF, BF)),
        in_specs=[ANY] * (1 + len(pieces)),
        out_specs=(WHOLE,) * 4,
        scratch_shapes=[pltpu.VMEM((hidden, width), BF)] * 3 + [pltpu.SemaphoreType.DMA((6,))],
        compiler_params=room(46),
        cost_estimate=expert_cost(rows, hidden, width),
    )(arrived, *pieces)


def expert_far(near, pieces, nodes):
    out_part, back_part, xs, gs = near
    rows, width = xs.shape
    hidden = len(pieces) * pieces[0].shape[1]
    scratch = [((rows, width), F32)] * 2 + [((hidden, width), BF)] * 3 + [((rows, width), BF)] * 2
    return pl.pallas_call(
        functools.partial(expert_far_kernel, nodes, len(pieces)),
        name="expert_far",
        out_shape=jax.ShapeDtypeStruct((nodes * OUT1_ROWS, width), BF),
        in_specs=[WHOLE] * 2 + [ANY] * (2 + len(pieces)),
        out_specs=ANY,
        scratch_shapes=[pltpu.VMEM(s, t) for s, t in scratch] + [pltpu.SemaphoreType.DMA((8,))],
        compiler_params=room(61),
        cost_estimate=expert_cost(rows, hidden, width),
    )(on_chip(xs), on_chip(gs), out_part, back_part, *pieces)


def weighted_hot(places, values, rows):
    ids = lax.broadcasted_iota(jnp.int32, (places.shape[0], rows), 1)
    total = jnp.zeros(ids.shape, F32)
    for k in range(TOP):
        total = total + jnp.where(places[:, k : k + 1] == ids, values[:, k : k + 1], 0.0)
    return total.astype(BF)


def weight_grads(table, places):
    ids = lax.broadcasted_iota(jnp.int32, table.shape, 1)
    lane = lax.broadcasted_iota(jnp.int32, (table.shape[0], 128), 1)
    result = jnp.zeros(lane.shape, F32)
    for k in range(TOP):
        column = jnp.sum(jnp.where(places[:, k : k + 1] == ids, table, 0.0), axis=1, keepdims=True)
        result = result + jnp.where(lane == k, column, 0.0)
    return jnp.transpose(result)[:8]


COLUMNS = 512


def sweep(home, hot, grads, table, use):
    matrix = hot[...]
    table[...] = jnp.zeros_like(table)

    def block(c, carry):
        cols = pl.ds(pl.multiple_of(c * COLUMNS, COLUMNS), COLUMNS)
        rows = home[:, cols]
        use(cols, jnp.dot(matrix, rows, preferred_element_type=F32))
        part = by_hidden(grads[:, cols], rows)
        table[...] += part
        return carry

    lax.fori_loop(0, home.shape[1] // COLUMNS, block, 0)


def combine_other_kernel(home, places, values, mix):
    matrix = weighted_hot(places[...], values[...], home.shape[0])
    mix[...] = jnp.dot(matrix, home[...], preferred_element_type=F32).astype(BF)


def grads_other_kernel(home, places, grads, dw):
    table = by_hidden(grads[...], home[...])
    dw[...] = weight_grads(table, places[: grads.shape[0]])


def combine_pair_kernel(home, places, values, grads, mix, dw, hot, table):
    toks = grads.shape[0]
    hot[...] = weighted_hot(places[...], values[...], home.shape[0])

    def use(cols, total):
        mix[:, cols] = total.astype(mix.dtype)

    sweep(home, hot, grads, table, use)
    dw[...] = weight_grads(table[...], places[:toks])


def combine_full_kernel(
    home, places, values, dw_own, dw_back, grads_at, own_at, returned_at, combined, d_tokens, d_weights, *scratch
):
    grads, own, returned, hot, table, sems = scratch
    toks = grads.shape[0]
    copies = [
        pltpu.make_async_copy(src, dst, sems.at[i])
        for i, (src, dst) in enumerate(((own_at, own), (returned_at, returned), (grads_at, grads)))
    ]
    for copy in copies:
        copy.start()
    hot[...] = weighted_hot(places[...], values[...], home.shape[0])
    for copy in copies:
        copy.wait()

    def use(cols, total):
        total = total + own[:, cols] + returned[:, cols].astype(F32)
        combined[:, cols] = total[:toks].astype(BF)
        d_tokens[:, cols] = total[toks:].astype(BF)

    sweep(home, hot, grads, table, use)
    d_weights[...] = (weight_grads(table[...], places[:toks]) + dw_own[...] + dw_back[...])[:TOP]


def combine_other(home, places, values):
    return pl.pallas_call(
        combine_other_kernel,
        name="combine_other",
        out_shape=jax.ShapeDtypeStruct((places.shape[0], home.shape[1]), BF),
        compiler_params=room(60),
        cost_estimate=pl.CostEstimate(
            flops=2 * places.shape[0] * home.shape[0] * home.shape[1], transcendentals=0, bytes_accessed=6 * 1024 * 1024
        ),
    )(home, places, values)


def grads_other_rows(home, places, grads):
    return pl.pallas_call(
        grads_other_kernel,
        name="grads_other",
        out_shape=jax.ShapeDtypeStruct((8, grads.shape[0]), F32),
        compiler_params=room(60),
        cost_estimate=pl.CostEstimate(
            flops=2 * grads.shape[0] * home.shape[0] * home.shape[1], transcendentals=0, bytes_accessed=6 * 1024 * 1024
        ),
    )(home, places, grads)


def combine_pair(home, places, values, grads, kind):
    toks, width = grads.shape
    return pl.pallas_call(
        combine_pair_kernel,
        out_shape=(jax.ShapeDtypeStruct((2 * toks, width), kind), jax.ShapeDtypeStruct((8, toks), F32)),
        scratch_shapes=[pltpu.VMEM((2 * toks, home.shape[0]), BF), pltpu.VMEM((toks, home.shape[0]), F32)],
        compiler_params=room(60),
        cost_estimate=pl.CostEstimate(
            flops=6 * toks * home.shape[0] * width, transcendentals=0, bytes_accessed=8 * 1024 * 1024
        ),
    )(home, places, values, grads)


def combine_full(home, places, values, grads, own, returned, dw_own, dw_back):
    toks, width = grads.shape
    return pl.pallas_call(
        combine_full_kernel,
        name="combine_full",
        out_shape=(
            jax.ShapeDtypeStruct((toks, width), BF),
            jax.ShapeDtypeStruct((toks, width), BF),
            jax.ShapeDtypeStruct((TOP, toks), F32),
        ),
        in_specs=[WHOLE] * 5 + [ANY] * 3,
        out_specs=(WHOLE,) * 3,
        scratch_shapes=[
            pltpu.VMEM((toks, width), BF),
            pltpu.VMEM((2 * toks, width), F32),
            pltpu.VMEM((2 * toks, width), BF),
            pltpu.VMEM((2 * toks, home.shape[0]), BF),
            pltpu.VMEM((toks, home.shape[0]), F32),
            pltpu.SemaphoreType.DMA((3,)),
        ],
        compiler_params=room(57),
        cost_estimate=pl.CostEstimate(
            flops=6 * toks * home.shape[0] * width, transcendentals=0, bytes_accessed=8 * 1024 * 1024
        ),
    )(on_chip(home), places, values, dw_own, dw_back, grads, own, returned)


def shards(tokens, route, combine_weights, w_gate, w_up, w_down, grad_out):
    nodes = lax.axis_size("node")
    planes = lax.axis_size("local")
    up = [(i, (i + 1) % planes) for i in range(planes)]
    down = [(i, (i - 1) % planes) for i in range(planes)]
    across = [(i, (i + 2) % planes) for i in range(planes)]

    def send(value, pairs):
        return lax.ppermute(value, "local", pairs)

    def exchange(rows):
        return lax.all_to_all(rows, "node", split_axis=0, concat_axis=0, tiled=True)

    tokens_other, grads_other = send(tokens, across), send(grad_out, across)
    route_t = route.T
    weight_t = combine_weights.T
    small = send(jnp.concatenate([weight_t, route_t.astype(F32)], axis=0), across)
    weight_other = small[:TOP]
    route_other = small[TOP:].astype(jnp.int32)

    gate_t = jnp.swapaxes(w_gate, 1, 2)
    up_t = jnp.swapaxes(w_up, 1, 2)
    half = gate_t.shape[1] // 2

    def piece(expert, part):
        cut = slice(part * half, (part + 1) * half)
        return jnp.stack([gate_t[expert, cut], up_t[expert, cut], w_down[expert, cut]])

    p0a, p0b, p1a, p1b = piece(0, 0), piece(0, 1), piece(1, 0), piece(1, 1)
    w0 = [p0a, p0b, send(p0a, down), send(p0b, up)]
    below_b, above_a = send(p1b, up), send(p1a, down)
    below_a, above_b = send(p1a, up), send(p1b, down)
    pair1 = [p1a, p1b, below_b, above_a]
    near1 = pair1 + [below_a, above_b]
    far1 = [send(above_a, down), send(below_b, up)]

    slot_own, slot_other = slots_of(route_t), slots_of(route_other)

    own_rows = dispatch(dispatch_own_kernel, nodes * OWN_ROWS, route_t, tokens, grad_out)
    arrived = exchange(own_rows)
    other_rows = dispatch(
        dispatch_other_kernel, nodes * OTHER_ROWS, route_t, route_other, tokens, grad_out, tokens_other, grads_other
    )
    arrived_other = exchange(other_rows)

    arrived_other = on_chip(arrived_other)
    pair_rows = expert_pair(arrived, arrived_other, w0, nodes)
    rows0 = expert_ninth(arrived_other, pair_rows, pair1, nodes)
    home0 = exchange(rows0)
    near = expert_near(arrived, near1, nodes)
    rows1 = expert_far(near, far1, nodes)
    home1 = exchange(rows1)

    def pair_place(route_rows, slot, main, rest):
        odd = route_rows % 2
        ninth = slot == 8
        index = jnp.where(ninth, rest + 4 * odd, main + slot)
        return jnp.where((odd == 0) | ninth, (route_rows // 2) * OUT0_ROWS + index, -1)

    def home_place(main, rest):
        return pair_place(route_t, slot_own, main, rest)

    def other_place(main, rest):
        return pair_place(route_other, slot_other, main, rest)

    def full_place(main):
        kept = (route_t % 2 == 1) & (slot_own < 8)
        return jnp.where(kept, (route_t // 2) * OUT1_ROWS + main + slot_own, -1)

    def stacked(*parts):
        return jnp.concatenate([p.T for p in parts], axis=0)

    places0 = stacked(home_place(0, 32), home_place(16, 34))
    places_other = stacked(other_place(8, 33), other_place(24, 35))
    places1 = stacked(full_place(0), full_place(8))
    values0, values_other = stacked(weight_t, weight_t), stacked(weight_other, weight_other)
    back = combine_other(home0, places_other, values_other)
    returned = send(back, across)
    dw_other = grads_other_rows(home0, places_other, grads_other)
    dw_back = send(dw_other, across)
    kept, dw_own = combine_pair(home0, places0, values0, grad_out, F32)
    combined, d_tokens, d_weights_t = combine_full(home1, places1, values0, grad_out, kept, returned, dw_own, dw_back)
    return combined, d_tokens, d_weights_t.T


def solution(mesh):
    tokens_spec = P(("node", "local"), None)

    return jax.shard_map(
        shards,
        mesh=mesh,
        in_specs=(
            tokens_spec,
            tokens_spec,
            tokens_spec,
            P("node", None, "local"),
            P("node", None, "local"),
            P("node", "local", None),
            tokens_spec,
        ),
        out_specs=(tokens_spec, tokens_spec, tokens_spec),
        check_vma=False,
    )
```
